32 devices in a mesh: groups: 2 (over y), wide: 4 (over z), narrow: 4 (over x, core).
Axes of the slice: x: 2, y: 2, z: 4, core: 2. Of those that a mesh axis runs over, the one named last changes fastest.
Arguments:
- tokens: bfloat16 [512, 4096], P(('groups', 'wide'), 'narrow'), parts along dimension 0, may hold values from -6 to 6
- routes: int32 [512, 8], P(('groups', 'wide')), parts along dimension 0, may hold values from 0 to 15, all different within a row; in each aligned block of 64 rows (0 to 63, 64 to 127, ...) at most 40 rows name the same one
- gate_weights: float32 [512, 8], P(('groups', 'wide')), parts along dimension 0, may hold values from 0.05 to 1
- delta_of: int32 [16], replicated, may hold values from 0 to 15, each once
- base_gate: bfloat16 [4096, 1536], P('wide', 'narrow'), may hold values from -0.09375 to 0.09375
- base_up: bfloat16 [4096, 1536], P('wide', 'narrow'), may hold values from -0.09375 to 0.09375
- base_down: bfloat16 [1536, 4096], P('wide', 'narrow'), may hold values from -0.15625 to 0.15625
- gate_left: bfloat16 [16, 4096, 32], P('wide', 'narrow'), may hold values from -0.09375 to 0.09375
- gate_right: bfloat16 [16, 32, 1536], P('wide', None, 'narrow'), may hold values from -0.5 to 0.5
- up_left: bfloat16 [16, 4096, 32], P('wide', 'narrow'), may hold values from -0.09375 to 0.09375
- up_right: bfloat16 [16, 32, 1536], P('wide', None, 'narrow'), may hold values from -0.5 to 0.5
- down_left: bfloat16 [16, 1536, 32], P('wide', 'narrow'), may hold values from -0.15625 to 0.15625
- down_right: bfloat16 [16, 32, 4096], P('wide', None, 'narrow'), may hold values from -0.5 to 0.5
Outputs:
- mixed_out: bfloat16 [512, 4096], P(('groups', 'wide'), 'narrow'), parts along dimension 0
The draws below stay inside these ranges and needn't reach their ends.
There are 2 independent parts, one for each index of `groups`. The reference program is written for one: setup_inputs(seed, part) draws one part's arguments, and reference() takes and returns one part's arrays. A program takes and returns all parts, laid end to end along the dimension named above; an argument that names none is the same for every part. Nothing has to cross between parts.
Inputs may be any that keep to these rules, and one draw needn't show every extreme that they name: `routes`: in each aligned block of 64 rows (the rows of one index of wide) no expert is named by more than 40 rows, and in some block some expert is named by exactly 40 rows.
All inputs are finite; a program needn't handle non-finite values.
Results may differ from the reference program's by a relative error of at most 0.0053.
Values may be sent and summed in bfloat16 or wider, within the bound.
A program may use at most 64 MiB of HBM per device.

```python
import math
import jax
import jax.numpy as jnp
import numpy as np
from jax import lax

D = 4096
FF = 1536
R = 32
TOP = 8
BLK = 64
EXPERTS = 16
TOKENS = 256
CAP = 40


def steps_of(rng, extent, shards, least, high):
    gain, own = 1.0, jax.random.fold_in(rng, 6)
    for position, shards_of in shards:
        heights = jnp.exp(jax.random.uniform(jax.random.fold_in(own, position), (shards_of,), jnp.float32, least / len(shards), high / len(shards)))
        gain = gain * jnp.repeat(heights, extent[position] // shards_of).reshape([-1 if axis == position else 1 for axis in range(len(extent))])
    return gain


def deal_out(own_key, own, number, rows, count, top, bound, lean):
    order = jax.random.permutation(own_key, count)
    crowded, common = portions_of(count, rows * top, bound, lean, True), portions_of(count, rows * top, bound, lean, False)
    places = jnp.arange(count)

    def named(lengths, rotation):
        used = int((lengths > 0).sum())
        fixed = max(1, used // 4)
        moved = fixed + (places - fixed + rotation * (used - fixed)) % max(1, count - fixed)
        return jnp.zeros((count,), jnp.int32).at[order[jnp.where(places < fixed, places, moved)]].set(jnp.asarray(lengths, jnp.int32))

    lengths = jnp.where(number % 4 == 0, named(crowded, number // 4), named(common, number - number // 4 - 1))
    mixed = jax.random.permutation(jax.random.fold_in(own, 3), count)
    giver, sink = mixed[0:count // 2 * 2:2], mixed[1:count // 2 * 2:2]
    slack = jnp.minimum(lengths[giver] - 1, bound - lengths[sink]) // 2
    slack = jnp.where((giver == order[0]) | (sink == order[0]) | (lengths[sink] == 0), 0, jnp.maximum(slack, 0))
    moved = jax.random.randint(jax.random.fold_in(own, 4), (count // 2,), 0, 1 << 20) % (slack + 1)
    lengths = lengths.at[giver].add(-moved).at[sink].add(moved)
    items = jnp.searchsorted(jnp.cumsum(lengths), jnp.arange(rows * top), side="right").astype(jnp.int32)
    table = items.reshape(top, rows).T
    table = table[jax.random.permutation(jax.random.fold_in(own, 1), rows)]
    rotation = jax.random.randint(jax.random.fold_in(own, 2), (rows, 1), 0, top)
    return jnp.take_along_axis(table, (jnp.arange(top)[None, :] + rotation) % top, axis=1)


def portions_of(count, total, most, lean, full):
    portions = [(1 << 20) // math.isqrt(rank ** lean) + 1 for rank in range(1, count + 1)]
    largest = most if full else min(most, max(-(-total // count), total * portions[0] // sum(portions)))
    least = 1 if total - largest >= count - 1 else 0
    given, surplus = [largest] + [least] * (count - 1), total - largest - least * (count - 1)
    while surplus > 0:
        free = [i for i in range(1, count) if given[i] < largest] or [i for i in range(1, count) if given[i] < most]
        whole, remaining = sum([portions[i] for i in free]), surplus
        for i in free:
            more = min(most - given[i], max(1, remaining * portions[i] // whole), surplus)
            given[i] = given[i] + more
            surplus = surplus - more
    return np.array(given)


def gaussian(rng, dims, width, bound, split=(), kind=jnp.bfloat16):
    array = width * jax.random.normal(rng, dims, jnp.float32)
    if split:
        array = array * steps_of(rng, dims, split, -0.22, 0.18)
    return jnp.clip(array, -bound, bound).astype(kind)


def setup_inputs(seed: int = 0, part: int = 0) -> dict:
    arg_keys = jax.random.split(jax.random.key(seed), 14)
    part_splits = jax.random.split(jax.random.fold_in(arg_keys[13], part), 14)
    tokens = gaussian(part_splits[0], (TOKENS, D), 1.0, 6.0, ((0, 4), (1, 4)))
    routes_keys = jax.random.split(jax.random.fold_in(part_splits[1], 1), TOKENS // BLK)
    routes_turns = jax.random.permutation(jax.random.fold_in(part_splits[1], 3), TOKENS // BLK)
    routes = jax.vmap(lambda own, number: deal_out(jax.random.fold_in(part_splits[1], 2), own, number, BLK, EXPERTS, TOP, CAP, 2))(routes_keys, routes_turns).reshape((TOKENS, TOP))
    gate_weights = jnp.clip(0.05 + 0.95 * jax.random.uniform(part_splits[2], (TOKENS, TOP), jnp.float32) ** steps_of(part_splits[2], (TOKENS, TOP), ((0, 4),), -0.2, 0.2), 0.05, 1.0)
    delta_of = jax.random.permutation(arg_keys[3], EXPERTS).astype(jnp.int32)
    base_gate = gaussian(arg_keys[4], (D, FF), D ** -0.5, 0.09375, ((0, 4), (1, 4)))
    base_up = gaussian(arg_keys[5], (D, FF), D ** -0.5, 0.09375, ((0, 4), (1, 4)))
    base_down = gaussian(arg_keys[6], (FF, D), FF ** -0.5, 0.15625, ((0, 4), (1, 4)))
    gate_left = gaussian(arg_keys[7], (EXPERTS, D, R), D ** -0.5, 0.09375, ((0, 4), (1, 4)))
    gate_right = gaussian(arg_keys[8], (EXPERTS, R, FF), (4 * R) ** -0.5, 0.5, ((0, 4), (2, 4)))
    up_left = gaussian(arg_keys[9], (EXPERTS, D, R), D ** -0.5, 0.09375, ((0, 4), (1, 4)))
    up_right = gaussian(arg_keys[10], (EXPERTS, R, FF), (4 * R) ** -0.5, 0.5, ((0, 4), (2, 4)))
    down_left = gaussian(arg_keys[11], (EXPERTS, FF, R), FF ** -0.5, 0.15625, ((0, 4), (1, 4)))
    down_right = gaussian(arg_keys[12], (EXPERTS, R, D), (4 * R) ** -0.5, 0.5, ((0, 4), (2, 4)))
    return {"tokens": tokens, "routes": routes, "gate_weights": gate_weights, "delta_of": delta_of, "base_gate": base_gate, "base_up": base_up, "base_down": base_down, "gate_left": gate_left, "gate_right": gate_right, "up_left": up_left, "up_right": up_right, "down_left": down_left, "down_right": down_right}


def rebuild(base, left, right):
    return (base.astype(jnp.float32) + jnp.dot(left, right, preferred_element_type=jnp.float32)).astype(jnp.bfloat16)


def reference(tokens, routes, gate_weights, delta_of, base_gate, base_up, base_down, gate_left, gate_right, up_left, up_right, down_left, down_right):
    token_count = tokens.shape[0]
    experts = delta_of.shape[0]
    expert_ids = jnp.arange(experts, dtype=jnp.int32)
    onehot = (routes[:, :, None] == expert_ids[None, None, :]).astype(jnp.int32)
    routed = jnp.sum(onehot, axis=1)
    blocked = routed.reshape(token_count // BLK, BLK, experts)
    before = (jnp.cumsum(blocked, axis=1) - blocked).reshape(token_count, experts)
    place_in = jnp.sum(onehot * before[:, None, :], axis=2).astype(jnp.int32)
    block_of = (jnp.arange(token_count, dtype=jnp.int32) // BLK)[:, None]
    slot_count = (token_count // BLK) * CAP
    flat_index = (routes * slot_count + block_of * CAP + place_in).reshape(-1).astype(jnp.int32)
    token_ids = jnp.repeat(jnp.arange(token_count, dtype=jnp.int32), routes.shape[1])
    source = jnp.full((experts * slot_count,), token_count, jnp.int32).at[flat_index].set(token_ids).reshape(experts, slot_count)
    scales = jnp.zeros((experts * slot_count,), jnp.float32).at[flat_index].set(gate_weights.reshape(-1).astype(jnp.float32)).reshape(experts, slot_count)
    padded = jnp.concatenate([tokens, jnp.zeros((1, tokens.shape[1]), tokens.dtype)], axis=0)

    def visit(running, inputs):
        expert, row_ids, row_scales = inputs
        delta_id = delta_of[expert]
        w_gate = rebuild(base_gate, gate_left[delta_id], gate_right[delta_id])
        w_up = rebuild(base_up, up_left[delta_id], up_right[delta_id])
        w_down = rebuild(base_down, down_left[delta_id], down_right[delta_id])
        rows_in = padded[row_ids]
        gate_act = jnp.dot(rows_in, w_gate, preferred_element_type=jnp.float32)
        up_act = jnp.dot(rows_in, w_up, preferred_element_type=jnp.float32)
        hidden = (jax.nn.silu(gate_act) * up_act).astype(jnp.bfloat16)
        result = jnp.dot(hidden, w_down, preferred_element_type=jnp.float32).astype(jnp.bfloat16)
        running = running.at[row_ids].add(row_scales[:, None] * result.astype(jnp.float32))
        return running, None

    start_sum = jnp.zeros((token_count + 1, tokens.shape[1]), jnp.float32)
    running, unused = lax.scan(visit, start_sum, (expert_ids, source, scales))
    return running[:token_count].astype(jnp.bfloat16)
```

```python
import jax
import jax.numpy as jnp
from jax import lax
from jax.experimental import pallas as pl
from jax.experimental.pallas import tpu as pltpu
from jax.sharding import PartitionSpec as P


def dot32(a, b):
    return jnp.dot(a, b, preferred_element_type=jnp.float32)


def dot32t(a, b):
    return lax.dot_general(a, b, (((1,), (1,)), ((), ())), preferred_element_type=jnp.float32)


PLANE = 4

LANES = 128


ORDER = (1, 2, 0, 3)


def kernel(
    tok, routes_hbm, shares_hbm, delta, bg_hbm, bu_hbm, bd_hbm, gl_hbm, gr_hbm, ul_hbm, ur_hbm, dl_hbm, dr_hbm, out,
    routes, shares, bgu, lefts, bd, dr, gr, ur, dl,
    xcol, xw, wts, gpart, gsend, grecv, gxs, gxr, gall, apart, asend, arecv, afin,
    hst, hacc, hsend, hlo, hhi, hpl, bpart, bsend, brecv, bfin, osend, orecv, oown,
    ti_s, to_s, tok_r, wt_s, wt_r, bs_s, bs_r, g_s, g_r, x_s, x_r, f_s, f_r, a_s, a_r,
    h_s, hl_r, hh_r, hb_s, hb_r, b_s, b_r, o_s, o_r, in_s,
):
    bf16, f32 = jnp.bfloat16, jnp.float32
    count = PLANE
    w, n = lax.axis_index("wide"), lax.axis_index("narrow")
    rows = tok.shape[0]
    span, cols = gr.shape
    exp_here = delta.shape[0] // count
    rank = span // exp_here
    chunk = LANES if cols % LANES == 0 else cols
    chunks = cols // chunk
    side = w // 2
    sign = 1 - 2 * side

    def mir(j):
        return j + side * (3 - 2 * j)

    depth = mir(w)
    inner = depth == 1
    end = depth == 0
    root = n == w
    relay = n == lax.rem(w + 2, count)
    pair = n + 1 - 2 * lax.rem(n, 2)
    across = lax.rem(n + 2, count)
    inward = w + sign
    buddy = w + 1 - 2 * lax.rem(w, 2)

    def up_of(d):
        return lax.rem(w + d, count)

    pairs = [
        (tok, xcol.at[w]), (routes_hbm, routes), (shares_hbm, shares),
    ]
    for c in range(chunks):
        for k, base in enumerate((bg_hbm, bu_hbm)):
            pairs.append((base.at[:, pl.ds(c * chunk, chunk)], bgu.at[:, pl.ds((2 * c + k) * chunk, chunk)]))
    first = len(pairs)
    pairs += [(gl_hbm, lefts.at[pl.ds(0, span)]), (ul_hbm, lefts.at[pl.ds(span, span)])]
    second = len(pairs)
    pairs += [(gr_hbm, gr), (ur_hbm, ur), (dl_hbm, dl)]
    third = len(pairs)
    pairs += [(bd_hbm, bd), (dr_hbm, dr)]
    loads = [pltpu.make_async_copy(a, b, in_s.at[i]) for i, (a, b) in enumerate(pairs)]

    def copy(src, dst, ss, rs, axis, peer):
        return pltpu.make_async_remote_copy(
            src_ref=src, dst_ref=dst, send_sem=ss, recv_sem=rs,
            device_id={axis: peer}, device_id_type=pl.DeviceIdType.MESH,
        )

    barrier = pltpu.get_barrier_semaphore()
    for d in range(1, count):
        pl.semaphore_signal(barrier, inc=1, device_id={"wide": up_of(d)}, device_id_type=pl.DeviceIdType.MESH)
    for peer in (pair, across):
        pl.semaphore_signal(barrier, inc=1, device_id={"narrow": peer}, device_id_type=pl.DeviceIdType.MESH)
    for load in loads:
        load.start()
    pl.semaphore_wait(barrier, count + 1)

    own_in = copy(tok, xcol.at[w], ti_s.at[0], tok_r.at[w], "wide", inward)
    own_out = copy(tok, xcol.at[w], to_s.at[0], tok_r.at[w], "wide", buddy)

    def tok_in(b):
        return copy(xcol.at[b], xcol.at[b], ti_s.at[1], tok_r.at[b], "wide", inward)

    def tok_out(b, k):
        return copy(xcol.at[b], xcol.at[b], to_s.at[k], tok_r.at[b], "wide", buddy)

    def pair_copy(b, src):
        return copy(src, xw.at[b], bs_s.at[b, 0], bs_r.at[b], "narrow", pair)

    def across_copy(b, src):
        return copy(src, xw.at[b], bs_s.at[b, 1], bs_r.at[b], "narrow", across)

    def wt_copy(d):
        return copy(wts.at[w], wts.at[w], wt_s.at[d], wt_r.at[w], "wide", up_of(d))

    def wt_from(d):
        return copy(wts.at[up_of(d)], wts.at[up_of(d)], wt_s.at[d], wt_r.at[up_of(d)], "wide", up_of(d))

    own_in.start()

    @pl.when(jnp.logical_and(inner, jnp.logical_not(root)))
    def _():
        own_out.start()

    @pl.when(root)
    def _():
        across_copy(w, tok).start()
        pair_copy(w, tok).start()

    for load in loads[:3]:
        load.wait()
    named, ids = routes[...], jnp.zeros(routes.shape, jnp.int32)
    for e in range(delta.shape[0]):
        ids = jnp.where(named == e, delta[e], ids)
    sets = lax.broadcasted_iota(jnp.int32, wts.shape[1:], 0)
    table = jnp.zeros(sets.shape, f32)
    for k in range(routes.shape[0]):
        table = table + jnp.where(sets == ids[k : k + 1], shares[k : k + 1, :], 0.0)
    wts[w] = table

    @pl.when(root)
    def _():
        xw[w] = xcol[w]

    for load in loads[3:first]:
        load.wait()

    def part_of(c):
        return pl.ds(2 * c * chunk, 2 * chunk)

    def g_copy(b, c):
        return copy(gsend.at[b, :, part_of(c)], grecv.at[b, :, part_of(c)], g_s.at[b, c], g_r.at[b, c], "wide", buddy)

    def x_copy(b, c):
        return copy(gxs.at[b, :, part_of(c)], gxr.at[b, :, part_of(c)], x_s.at[b, c], x_r.at[b, c], "wide", inward)

    def f_copy(b, c):
        return copy(gall.at[b, :, part_of(c)], gall.at[b, :, part_of(c)], f_s.at[b, c], f_r.at[b, c], "wide", buddy)

    def arrive(j):
        b = mir(1 - depth) if j == 1 else mir(j)

        @pl.when(jnp.logical_or(root, inner))
        def _():
            tok_in(b).wait_recv()

        if j == 1:

            @pl.when(inner)
            def _():
                tok_in(b).start()

        else:

            @pl.when(jnp.logical_and(inner, jnp.logical_not(root)))
            def _():
                tok_out(b, j - 1).start()

        @pl.when(root)
        def _():
            across_copy(b, xcol.at[b]).start()
            pair_copy(b, xcol.at[b]).start()
            xw[b] = xcol[b]

    def base(j):
        b = w if j == 0 else (mir(1 - depth) if j == 1 else mir(j))

        @pl.when(jnp.logical_not(root))
        def _():
            pair_copy(b, xw.at[b]).wait_recv()

        @pl.when(relay)
        def _():
            pair_copy(b, xw.at[b]).start()

        both = dot32(xw[b], bgu[...])
        gpart[b] = both

        @pl.when(end)
        def _():
            gsend[b] = both.astype(bf16)
            for c in range(chunks):
                g_copy(b, c).start()

    def side_sum(j):
        b = mir(j)

        @pl.when(inner)
        def _():
            for c in range(chunks):
                part = slice(2 * c * chunk, 2 * (c + 1) * chunk)
                g_copy(b, c).wait_recv()
                total = gpart[b, :, part] + grecv[b, :, part].astype(f32)
                gpart[b, :, part] = total
                gxs[b, :, part] = total.astype(bf16)
                x_copy(b, c).start()

    base(0)
    arrive(1)
    arrive(2)
    base(1)
    arrive(3)
    base(2)
    base(3)

    @pl.when(jnp.logical_and(inner, root))
    def _():
        own_out.start()
        tok_out(mir(2), 1).start()
        tok_out(mir(3), 2).start()

    for d in range(1, count):
        wt_copy(d).start()
    side_sum(0)
    side_sum(1)

    @pl.when(jnp.logical_and(end, jnp.logical_not(root)))
    def _():
        for j in range(1, count):
            tok_in(mir(j)).wait_recv()

    for load in loads[first:second]:
        load.wait()

    def a_copy(k):
        return copy(asend.at[k], arecv.at[k], a_s.at[k], a_r.at[k], "narrow", (pair, across)[k])

    for b in range(count):
        apart[b] = dot32t(xcol[b], lefts[...])
    asend[0] = apart[...].astype(bf16)
    a_copy(0).start()
    side_sum(2)
    a_copy(0).wait_recv()
    apart[...] = apart[...] + arecv[0].astype(f32)
    asend[1] = apart[...].astype(bf16)
    a_copy(1).start()
    side_sum(3)
    for load in loads[second:third]:
        load.wait()
    for d in range(1, count):
        wt_from(d).wait_recv()

    def settle(b):
        @pl.when(inner)
        def _():
            for c in range(chunks):
                part = slice(2 * c * chunk, 2 * (c + 1) * chunk)
                x_copy(b, c).wait_recv()
                total = gpart[b, :, part] + gxr[b, :, part].astype(f32)
                gpart[b, :, part] = total
                gall[b, :, part] = total.astype(bf16)
                f_copy(b, c).start()

    def fetch(b):
        @pl.when(end)
        def _():
            for c in range(chunks):
                part = slice(2 * c * chunk, 2 * (c + 1) * chunk)
                f_copy(b, c).wait_recv()
                gpart[b, :, part] = gall[b, :, part].astype(f32)

    groups_of = lax.broadcasted_iota(jnp.int32, (rows, span), 1) // rank

    def spread(block):
        return jnp.concatenate(
            [jnp.where(groups_of == e, block, jnp.zeros_like(block)) for e in range(exp_here)], axis=0
        )

    def hidden_of(b):
        scales = wts[b].T
        ids = lax.broadcasted_iota(jnp.int32, scales.shape, 1)
        scale = [
            jnp.sum(jnp.where(ids == w * exp_here + e, scales, 0.0), axis=1, keepdims=True) for e in range(exp_here)
        ]
        thin_gate, thin_up = spread(afin[b, :, :span]), spread(afin[b, :, span:])
        for c in range(chunks):
            part = slice(c * chunk, (c + 1) * chunk)
            gates = gpart[b, :, 2 * c * chunk : (2 * c + 1) * chunk]
            ups = gpart[b, :, (2 * c + 1) * chunk : 2 * (c + 1) * chunk]
            more_gate, more_up = dot32(thin_gate, gr[:, part]), dot32(thin_up, ur[:, part])
            acc = None
            for e in range(exp_here):
                own = slice(e * rows, (e + 1) * rows)
                gate, up = gates + more_gate[own], ups + more_up[own]
                hidden = gate / (1.0 + jnp.exp(-gate)) * up * scale[e]
                acc = hidden if acc is None else acc + hidden
                hst[own, part] = hidden.astype(bf16)
            hacc[b, :, part] = acc
        thin = dot32t(hst[...], dl[...])
        mixed = jnp.zeros((rows, span), f32)
        for e in range(exp_here):
            mixed = mixed + jnp.where(groups_of == e, thin[e * rows : (e + 1) * rows], 0.0)
        bpart[b] = mixed

    def up_copy(b):
        return copy(hsend.at[b], hlo.at[b], h_s.at[b], hl_r.at[b], "wide", lax.rem(w + 1, count))

    def down_copy(b):
        return copy(hsend.at[b], hhi.at[b], h_s.at[b], hh_r.at[b], "wide", lax.rem(w + count - 1, count))

    def pass_on(b):
        @pl.when(w < n)
        def _():
            @pl.when(w > 0)
            def _():
                up_copy(b).wait_recv()
                hacc[b] = hacc[b] + hlo[b].astype(f32)

            hsend[b] = hacc[b].astype(bf16)
            up_copy(b).start()

        @pl.when(w > n)
        def _():
            @pl.when(w < count - 1)
            def _():
                down_copy(b).wait_recv()
                hacc[b] = hacc[b] + hhi[b].astype(f32)

            hsend[b] = hacc[b].astype(bf16)
            down_copy(b).start()

    def hpair(b):
        return copy(hpl.at[b], hpl.at[b], hb_s.at[0, b], hb_r.at[b], "narrow", pair)

    def hacross(b):
        return copy(hpl.at[b], hpl.at[b], hb_s.at[1, b], hb_r.at[b], "narrow", across)

    def collect(b):
        @pl.when(root)
        def _():
            @pl.when(w > 0)
            def _():
                up_copy(b).wait_recv()
                hacc[b] = hacc[b] + hlo[b].astype(f32)

            @pl.when(w < count - 1)
            def _():
                down_copy(b).wait_recv()
                hacc[b] = hacc[b] + hhi[b].astype(f32)

            hpl[b] = hacc[b].astype(bf16)
            hacross(b).start()
            hpair(b).start()

    settle(ORDER[0])
    settle(ORDER[1])
    a_copy(1).wait_recv()
    afin[...] = (apart[...] + arecv[1].astype(f32)).astype(bf16)
    for i in range(count):
        fetch(ORDER[i])
        hidden_of(ORDER[i])
        if i + 2 < count:
            settle(ORDER[i + 2])
        if i > 0:
            pass_on(ORDER[i - 1])

    def b_copy(k):
        return copy(bsend.at[k], brecv.at[k], b_s.at[k], b_r.at[k], "narrow", (pair, across)[k])

    bsend[0] = bpart[...].astype(bf16)
    b_copy(0).start()
    pass_on(ORDER[-1])
    for b in ORDER[:-1]:
        collect(b)
    b_copy(0).wait_recv()
    bpart[...] = bpart[...] + brecv[0].astype(f32)
    bsend[1] = bpart[...].astype(bf16)
    b_copy(1).start()
    collect(ORDER[-1])
    for load in loads[third:]:
        load.wait()
    b_copy(1).wait_recv()
    bfin[...] = (bpart[...] + brecv[1].astype(f32)).astype(bf16)

    def o_copy(b):
        return copy(osend.at[b], orecv.at[w], o_s.at[b], o_r.at[w], "wide", b)

    def o_from(s):
        return copy(osend.at[s], orecv.at[s], o_s.at[s], o_r.at[s], "wide", s)

    for b in ORDER:

        @pl.when(jnp.logical_not(root))
        def _():
            hpair(b).wait_recv()

        @pl.when(relay)
        def _():
            hpair(b).start()

        part = dot32(hpl[b], bd[...]) + dot32(bfin[b], dr[...])

        @pl.when(w == b)
        def _():
            oown[...] = part

        @pl.when(w != b)
        def _():
            osend[b] = part.astype(bf16)
            o_copy(b).start()

    total = oown[...]
    for d in range(1, count):
        s = up_of(d)
        o_from(s).wait_recv()
        total = total + orecv[s].astype(f32)
    out[...] = total.astype(bf16)

    own_in.wait_send()
    for d in range(1, count):
        wt_copy(d).wait_send()
        o_from(up_of(d)).wait_send()
    for k in range(2):
        a_copy(k).wait_send()
        b_copy(k).wait_send()

    @pl.when(inner)
    def _():
        own_out.wait_send()
        tok_in(mir(0)).wait_send()
        for j in (2, 3):
            tok_out(mir(j), j - 1).wait_send()
        for b in range(count):
            for c in range(chunks):
                x_copy(b, c).wait_send()
                f_copy(b, c).wait_send()

    @pl.when(end)
    def _():
        for b in range(count):
            for c in range(chunks):
                g_copy(b, c).wait_send()

    @pl.when(root)
    def _():
        for b in range(count):
            across_copy(b, xcol.at[b]).wait_send()
            pair_copy(b, xcol.at[b]).wait_send()
            hacross(b).wait_send()
            hpair(b).wait_send()

    @pl.when(relay)
    def _():
        for b in range(count):
            pair_copy(b, xw.at[b]).wait_send()
            hpair(b).wait_send()

    @pl.when(jnp.logical_not(root))
    def _():
        for b in range(count):
            up_copy(b).wait_send()


def fused(tokens, routes, shares, delta, bg, bu, bd, gl, gr, ul, ur, dl, dr):
    bf16, f32 = jnp.bfloat16, jnp.float32
    count = PLANE
    rows, feats = tokens.shape
    depth, cols = bg.shape
    exp_here, rank, _ = gr.shape
    span = exp_here * rank
    sets = -(-delta.shape[0] // 8) * 8
    chunks = cols // LANES if cols % LANES == 0 else 1
    sem = pltpu.SemaphoreType.DMA
    vm = pltpu.VMEM
    out_feats = bd.shape[1]
    top = routes.shape[1]
    hbm = pl.BlockSpec(memory_space=pl.ANY)
    four = sem((count,))
    grid4 = sem((count, chunks))
    return pl.pallas_call(
        kernel,
        out_shape=jax.ShapeDtypeStruct((rows, out_feats), bf16),
        in_specs=[hbm, hbm, hbm, pl.BlockSpec(memory_space=pltpu.SMEM)] + [hbm] * 9,
        out_specs=pl.BlockSpec(memory_space=pltpu.VMEM),
        scratch_shapes=[
            vm((top, rows), jnp.int32), vm((top, rows), f32),
            vm((depth, 2 * cols), bf16),
            vm((2 * span, feats), bf16),
            vm(bd.shape, bf16),
            vm((span, out_feats), bf16),
            vm((span, cols), bf16), vm((span, cols), bf16), vm((span, cols), bf16),
            vm((count, rows, feats), bf16),
            vm((count, rows, feats), bf16),
            vm((count, sets, rows), f32),
            vm((count, rows, 2 * cols), f32),
            vm((count, rows, 2 * cols), bf16),
            vm((count, rows, 2 * cols), bf16),
            vm((count, rows, 2 * cols), bf16),
            vm((count, rows, 2 * cols), bf16),
            vm((count, rows, 2 * cols), bf16),
            vm((count, rows, 2 * span), f32),
            vm((2, count, rows, 2 * span), bf16),
            vm((2, count, rows, 2 * span), bf16),
            vm((count, rows, 2 * span), bf16),
            vm((exp_here * rows, cols), bf16),
            vm((count, rows, cols), f32),
            vm((count, rows, cols), bf16),
            vm((count, rows, cols), bf16),
            vm((count, rows, cols), bf16),
            vm((count, rows, cols), bf16),
            vm((count, rows, span), f32),
            vm((2, count, rows, span), bf16),
            vm((2, count, rows, span), bf16),
            vm((count, rows, span), bf16),
            vm((count, rows, out_feats), bf16),
            vm((count, rows, out_feats), bf16),
            vm((rows, out_feats), f32),
            sem((2,)), sem((3,)), four, four, four, sem((count, 2)), four,
            grid4, grid4, grid4, grid4, grid4, grid4, sem((2,)), sem((2,)),
            four, four, four, sem((2, count)), four, sem((2,)), sem((2,)), four, four, sem((10 + 2 * chunks,)),
        ],
        compiler_params=pltpu.CompilerParams(collective_id=0, has_side_effects=True, vmem_limit_bytes=60 * 1024 * 1024),
    )(
        tokens, routes.T, shares.T, delta, bg, bu, bd,
        jnp.swapaxes(gl, 1, 2).reshape(span, feats), gr.reshape(span, cols),
        jnp.swapaxes(ul, 1, 2).reshape(span, feats), ur.reshape(span, cols),
        jnp.swapaxes(dl, 1, 2).reshape(span, cols), dr.reshape(span, out_feats),
    )


def shards(
    tokens,
    routes,
    gate_weights,
    delta_of,
    base_gate,
    base_up,
    base_down,
    gate_left,
    gate_right,
    up_left,
    up_right,
    down_left,
    down_right,
):
    if lax.axis_size("narrow") == PLANE and lax.axis_size("wide") == PLANE:
        return fused(
            tokens, routes, gate_weights, delta_of, base_gate, base_up, base_down,
            gate_left, gate_right, up_left, up_right, down_left, down_right,
        )
    exp_here, _, rank = gate_left.shape
    experts = delta_of.shape[0]
    mine = lax.axis_index("wide")
    bf16 = jnp.bfloat16

    expert_ids = lax.broadcasted_iota(jnp.int32, (1, 1, experts), 2)
    named = routes[:, :, None] == expert_ids
    delta_ids = jnp.sum(jnp.where(named, delta_of[None, None, :], 0), axis=2)
    weight_of = jnp.sum(
        jnp.where(delta_ids[:, :, None] == expert_ids, gate_weights[:, :, None], 0.0), axis=1
    )
    weights = lax.all_gather(weight_of, "wide", axis=0, tiled=True)
    weights = lax.dynamic_slice_in_dim(weights, mine * exp_here, exp_here, axis=1)

    rows = lax.all_gather(tokens, "wide", axis=0, tiled=True)
    full = lax.all_gather(rows, "narrow", axis=1, tiled=True)
    depth = base_gate.shape[0]
    part = lax.dynamic_slice_in_dim(full, mine * depth, depth, axis=1)

    base_both = jnp.concatenate([base_gate, base_up], axis=1)
    both = lax.psum(dot32(part, base_both), "wide")
    columns = base_gate.shape[1]

    lefts = jnp.concatenate([gate_left, up_left], axis=0)
    low = lax.psum(jnp.einsum("td,edr->ter", rows, lefts, preferred_element_type=jnp.float32), "narrow")
    low = low.astype(bf16)

    mixed = 0.0
    thin = []
    for e in range(exp_here):
        gate = both[:, :columns] + dot32(low[:, e], gate_right[e])
        up = both[:, columns:] + dot32(low[:, exp_here + e], up_right[e])
        hidden = jax.nn.silu(gate) * up * weights[:, e : e + 1]
        mixed = mixed + hidden
        thin.append(dot32(hidden.astype(bf16), down_left[e]))
    mixed = lax.psum(mixed, "wide").astype(bf16)
    mixed_full = lax.all_gather(mixed, "narrow", axis=1, tiled=True)
    depth = base_down.shape[0]
    mixed_part = lax.dynamic_slice_in_dim(mixed_full, mine * depth, depth, axis=1)
    thin = lax.psum(jnp.concatenate(thin, axis=1), "narrow").astype(bf16)
    out = dot32(mixed_part, base_down) + dot32(thin, down_right.reshape(exp_here * rank, -1))
    out = lax.psum_scatter(out, "wide", scatter_dimension=0, tiled=True)
    return out.astype(bf16)


def solution(mesh):
    return jax.shard_map(
        shards,
        mesh=mesh,
        in_specs=(
            P(("groups", "wide"), "narrow"),
            P(("groups", "wide"), None),
            P(("groups", "wide"), None),
            P(),
            P("wide", "narrow"),
            P("wide", "narrow"),
            P("wide", "narrow"),
            P("wide", "narrow", None),
            P("wide", None, "narrow"),
            P("wide", "narrow", None),
            P("wide", None, "narrow"),
            P("wide", "narrow", None),
            P("wide", None, "narrow"),
        ),
        out_specs=P(("groups", "wide"), "narrow"),
        check_vma=False,
    )
```

```python
import jax
import jax.numpy as jnp
from jax import lax
from jax.experimental import pallas as pl
from jax.experimental.pallas import tpu as pltpu
from jax.sharding import PartitionSpec as P


def dot32(a, b):
    return jnp.dot(a, b, preferred_element_type=jnp.float32)


def dot32t(a, b):
    return lax.dot_general(a, b, (((1,), (1,)), ((), ())), preferred_element_type=jnp.float32)


PLANE = 4

LANES = 128


ORDER = (1, 2, 0, 3)


def kernel(
    tok, routes_hbm, shares_hbm, delta, bg_hbm, bu_hbm, bd_hbm, gl_hbm, gr_hbm, ul_hbm, ur_hbm, dl_hbm, dr_hbm, out,
    routes, shares, bgu, lefts, bd, dr, gr, ur, dl,
    xcol, xw, wts, gpart, gsend, grecv, gxs, gxr, gall, apart, asend, arecv,
    hst, hacc, hsend, hrecv, hpl, bpart, bsend, brecv, osend, orecv, oown,
    ti_s, to_s, tok_r, wt_s, wt_r, bs_s, bs_r, g_s, g_r, x_s, x_r, f_s, f_r, a_s, a_r,
    h_s, h_r, hb_s, hb_r, b_s, b_r, o_s, o_r, in_s,
):
    bf16, f32 = jnp.bfloat16, jnp.float32
    count = PLANE
    w, n = lax.axis_index("wide"), lax.axis_index("narrow")
    rows = tok.shape[0]
    span, cols = gr.shape
    exp_here = delta.shape[0] // count
    rank = span // exp_here
    chunk = LANES if cols % LANES == 0 else cols
    chunks = cols // chunk
    side = w // 2
    sign = 1 - 2 * side

    def mir(j):
        return j + side * (3 - 2 * j)

    depth = mir(w)
    inner = depth == 1
    end = depth == 0
    root = n == w
    relay = n == lax.rem(w + 2, count)
    pair = n + 1 - 2 * lax.rem(n, 2)
    across = lax.rem(n + 2, count)
    beside = (pair, across, lax.rem(pair + 2, count))
    inward = w + sign
    buddy = w + 1 - 2 * lax.rem(w, 2)

    def up_of(d):
        return lax.rem(w + d, count)

    pairs = [
        (tok, xcol.at[w]), (routes_hbm, routes), (shares_hbm, shares),
    ]
    pairs += [(gl_hbm, lefts.at[pl.ds(0, span)]), (ul_hbm, lefts.at[pl.ds(span, span)])]
    first = len(pairs)
    for c in range(chunks):
        for k, base in enumerate((bg_hbm, bu_hbm)):
            pairs.append((base.at[:, pl.ds(c * chunk, chunk)], bgu.at[:, pl.ds((2 * c + k) * chunk, chunk)]))
    second = len(pairs)
    pairs += [(gr_hbm, gr), (ur_hbm, ur), (dl_hbm, dl)]
    third = len(pairs)
    pairs += [(bd_hbm, bd), (dr_hbm, dr)]
    loads = [pltpu.make_async_copy(a, b, in_s.at[i]) for i, (a, b) in enumerate(pairs)]

    def copy(src, dst, ss, rs, axis, peer):
        return pltpu.make_async_remote_copy(
            src_ref=src, dst_ref=dst, send_sem=ss, recv_sem=rs,
            device_id={axis: peer}, device_id_type=pl.DeviceIdType.MESH,
        )

    barrier = pltpu.get_barrier_semaphore()
    for d in range(1, count):
        pl.semaphore_signal(barrier, inc=1, device_id={"wide": up_of(d)}, device_id_type=pl.DeviceIdType.MESH)
    for peer in beside:
        pl.semaphore_signal(barrier, inc=1, device_id={"narrow": peer}, device_id_type=pl.DeviceIdType.MESH)
    for load in loads:
        load.start()
    pl.semaphore_wait(barrier, 2 * (count - 1))

    own_in = copy(tok, xcol.at[w], ti_s.at[0], tok_r.at[w], "wide", inward)
    own_out = copy(tok, xcol.at[w], to_s.at[0], tok_r.at[w], "wide", buddy)

    own_far = copy(tok, xcol.at[w], ti_s.at[1], tok_r.at[w], "wide", count - 1 - buddy)

    def tok_in(b):
        return copy(xcol.at[b], xcol.at[b], ti_s.at[1], tok_r.at[b], "wide", buddy)

    def tok_out(b, k):
        return copy(xcol.at[b], xcol.at[b], to_s.at[k], tok_r.at[b], "wide", buddy)

    def pair_copy(b, src):
        return copy(src, xw.at[b], bs_s.at[b, 0], bs_r.at[b], "narrow", pair)

    def across_copy(b, src):
        return copy(src, xw.at[b], bs_s.at[b, 1], bs_r.at[b], "narrow", across)

    def wt_copy(d):
        return copy(wts.at[w], wts.at[w], wt_s.at[d], wt_r.at[w], "wide", up_of(d))

    def wt_from(d):
        return copy(wts.at[up_of(d)], wts.at[up_of(d)], wt_s.at[d], wt_r.at[up_of(d)], "wide", up_of(d))

    own_in.start()

    @pl.when(end)
    def _():
        own_far.start()

    @pl.when(jnp.logical_and(inner, jnp.logical_not(root)))
    def _():
        own_out.start()

    @pl.when(root)
    def _():
        across_copy(w, tok).start()
        pair_copy(w, tok).start()

    for load in loads[:3]:
        load.wait()
    named, ids = routes[...], jnp.zeros(routes.shape, jnp.int32)
    for e in range(delta.shape[0]):
        ids = jnp.where(named == e, delta[e], ids)
    sets = lax.broadcasted_iota(jnp.int32, wts.shape[1:], 0)
    table = jnp.zeros(sets.shape, f32)
    for k in range(routes.shape[0]):
        table = table + jnp.where(sets == ids[k : k + 1], shares[k : k + 1, :], 0.0)
    wts[w] = table

    @pl.when(root)
    def _():
        xw[w] = xcol[w]

    def a_copy(k, b):
        return copy(asend.at[b], arecv.at[k, b], a_s.at[k, b], a_r.at[k, b], "narrow", beside[k])

    def low(j):
        b = w if j == 0 else (mir(1 - depth) if j == 1 else mir(j))
        if j > 0:

            @pl.when(jnp.logical_and(end, jnp.logical_not(root)))
            def _():
                tok_in(b).wait_recv()

        thin = dot32t(xcol[b], lefts[...])
        apart[b] = thin
        asend[b] = thin.astype(bf16)
        for k in range(3):
            a_copy(k, b).start()

    for load in loads[3:first]:
        load.wait()
    low(0)
    for load in loads[first:second]:
        load.wait()

    def part_of(c):
        return pl.ds(2 * c * chunk, 2 * chunk)

    def g_copy(b, c):
        return copy(gsend.at[b, :, part_of(c)], grecv.at[b, :, part_of(c)], g_s.at[b, c], g_r.at[b, c], "wide", buddy)

    def x_copy(b, c):
        return copy(gxs.at[b, :, part_of(c)], gxr.at[b, :, part_of(c)], x_s.at[b, c], x_r.at[b, c], "wide", inward)

    def f_copy(b, c):
        return copy(gall.at[b, :, part_of(c)], gall.at[b, :, part_of(c)], f_s.at[b, c], f_r.at[b, c], "wide", buddy)

    def arrive(j, who):
        b = mir(1 - depth) if j == 1 else mir(j)

        @pl.when(jnp.logical_and(who, jnp.logical_or(root, inner)))
        def _():
            tok_in(b).wait_recv()

        if j > 1 and who is inner:

            @pl.when(jnp.logical_and(inner, jnp.logical_not(root)))
            def _():
                tok_out(b, j - 1).start()

            @pl.when(jnp.logical_and(inner, root))
            def _():
                if j == 2:
                    own_out.start()
                else:
                    tok_out(mir(2), 1).start()
                    tok_out(b, 2).start()

        @pl.when(jnp.logical_and(who, root))
        def _():
            across_copy(b, xcol.at[b]).start()
            pair_copy(b, xcol.at[b]).start()
            xw[b] = xcol[b]

    def base(j):
        b = w if j == 0 else (mir(1 - depth) if j == 1 else mir(j))

        @pl.when(jnp.logical_not(root))
        def _():
            pair_copy(b, xw.at[b]).wait_recv()

        @pl.when(relay)
        def _():
            pair_copy(b, xw.at[b]).start()

        both = dot32(xw[b], bgu[...])
        gpart[b] = both

        @pl.when(end)
        def _():
            gsend[b] = both.astype(bf16)
            for c in range(chunks):
                g_copy(b, c).start()

    def side_sum(j):
        b = mir(j)

        @pl.when(inner)
        def _():
            for c in range(chunks):
                part = slice(2 * c * chunk, 2 * (c + 1) * chunk)
                g_copy(b, c).wait_recv()
                total = gpart[b, :, part] + grecv[b, :, part].astype(f32)
                gpart[b, :, part] = total
                gxs[b, :, part] = total.astype(bf16)
                x_copy(b, c).start()

    base(0)
    for j in (1, 2, 3):
        arrive(j, inner)
    for j in (1, 2, 3):
        arrive(j, end)
        base(j)
    for d in range(1, count):
        wt_copy(d).start()
    side_sum(0)
    side_sum(1)
    low(1)
    low(2)
    low(3)
    side_sum(2)
    side_sum(3)
    for load in loads[second:]:
        load.wait()
    for d in range(1, count):
        wt_from(d).wait_recv()

    def settle(b):
        @pl.when(inner)
        def _():
            for c in range(chunks):
                part = slice(2 * c * chunk, 2 * (c + 1) * chunk)
                x_copy(b, c).wait_recv()
                total = gpart[b, :, part] + gxr[b, :, part].astype(f32)
                gpart[b, :, part] = total
                gall[b, :, part] = total.astype(bf16)
                f_copy(b, c).start()

    def fetch(b):
        @pl.when(end)
        def _():
            for c in range(chunks):
                part = slice(2 * c * chunk, 2 * (c + 1) * chunk)
                f_copy(b, c).wait_recv()
                gpart[b, :, part] = gall[b, :, part].astype(f32)

    groups_of = lax.broadcasted_iota(jnp.int32, (rows, span), 1) // rank

    def spread(block):
        return jnp.concatenate(
            [jnp.where(groups_of == e, block, jnp.zeros_like(block)) for e in range(exp_here)], axis=0
        )

    def b_copy(k, b):
        return copy(bsend.at[b], brecv.at[k, b], b_s.at[k, b], b_r.at[k, b], "narrow", beside[k])

    def hidden_of(b):
        scales = wts[b].T
        ids = lax.broadcasted_iota(jnp.int32, scales.shape, 1)
        scale = [
            jnp.sum(jnp.where(ids == w * exp_here + e, scales, 0.0), axis=1, keepdims=True) for e in range(exp_here)
        ]
        low_sum = apart[b]
        for k in range(3):
            a_copy(k, b).wait_recv()
            low_sum = low_sum + arecv[k, b].astype(f32)
        low_sum = low_sum.astype(bf16)
        thin_gate, thin_up = spread(low_sum[:, :span]), spread(low_sum[:, span:])
        for c in range(chunks):
            part = slice(c * chunk, (c + 1) * chunk)
            gates = gpart[b, :, 2 * c * chunk : (2 * c + 1) * chunk]
            ups = gpart[b, :, (2 * c + 1) * chunk : 2 * (c + 1) * chunk]
            more_gate, more_up = dot32(thin_gate, gr[:, part]), dot32(thin_up, ur[:, part])
            acc = None
            for e in range(exp_here):
                own = slice(e * rows, (e + 1) * rows)
                gate, up = gates + more_gate[own], ups + more_up[own]
                hidden = gate / (1.0 + jnp.exp(-gate)) * up * scale[e]
                acc = hidden if acc is None else acc + hidden
                hst[own, part] = hidden.astype(bf16)
            hacc[b, :, part] = acc
        thin = dot32t(hst[...], dl[...])
        mixed = jnp.zeros((rows, span), f32)
        for e in range(exp_here):
            mixed = mixed + jnp.where(groups_of == e, thin[e * rows : (e + 1) * rows], 0.0)
        bpart[b] = mixed
        bsend[b] = mixed.astype(bf16)
        for k in range(3):
            b_copy(k, b).start()

    def h_copy(b):
        return copy(hsend.at[b], hrecv.at[w, b], h_s.at[b], h_r.at[w, b], "wide", n)

    def h_from(k, b):
        return copy(hsend.at[b], hrecv.at[k, b], h_s.at[b], h_r.at[k, b], "wide", k)

    def pass_on(b):
        @pl.when(jnp.logical_not(root))
        def _():
            hsend[b] = hacc[b].astype(bf16)
            h_copy(b).start()

    def hpair(b):
        return copy(hpl.at[b], hpl.at[b], hb_s.at[0, b], hb_r.at[b], "narrow", pair)

    def hacross(b):
        return copy(hpl.at[b], hpl.at[b], hb_s.at[1, b], hb_r.at[b], "narrow", across)

    def collect(b):
        @pl.when(root)
        def _():
            whole = hacc[b]
            for d in range(1, count):
                h_from(up_of(d), b).wait_recv()
                whole = whole + hrecv[up_of(d), b].astype(f32)
            hpl[b] = whole.astype(bf16)
            hacross(b).start()
            hpair(b).start()

    def o_copy(b):
        return copy(osend.at[b], orecv.at[w], o_s.at[b], o_r.at[w], "wide", b)

    def o_from(k):
        return copy(osend.at[k], orecv.at[k], o_s.at[k], o_r.at[k], "wide", k)

    def project(b):
        @pl.when(jnp.logical_not(root))
        def _():
            hpair(b).wait_recv()

        @pl.when(relay)
        def _():
            hpair(b).start()

        thin = bpart[b]
        for k in range(3):
            b_copy(k, b).wait_recv()
            thin = thin + brecv[k, b].astype(f32)
        part = dot32(hpl[b], bd[...]) + dot32(thin.astype(bf16), dr[...])

        @pl.when(w == b)
        def _():
            oown[...] = part

        @pl.when(w != b)
        def _():
            osend[b] = part.astype(bf16)
            o_copy(b).start()

    settle(ORDER[0])
    settle(ORDER[1])
    for i in range(count):
        fetch(ORDER[i])
        hidden_of(ORDER[i])
        pass_on(ORDER[i])
        if i + 2 < count:
            settle(ORDER[i + 2])
    for b in ORDER:
        collect(b)
        project(b)
    total = oown[...]
    for d in range(1, count):
        k = up_of(d)
        o_from(k).wait_recv()
        total = total + orecv[k].astype(f32)
    out[...] = total.astype(bf16)

    own_in.wait_send()
    for d in range(1, count):
        wt_copy(d).wait_send()
        o_from(up_of(d)).wait_send()
    for k in range(3):
        for b in range(count):
            a_copy(k, b).wait_send()
            b_copy(k, b).wait_send()

    @pl.when(inner)
    def _():
        own_out.wait_send()
        for j in (2, 3):
            tok_out(mir(j), j - 1).wait_send()
        for b in range(count):
            for c in range(chunks):
                x_copy(b, c).wait_send()
                f_copy(b, c).wait_send()

    @pl.when(end)
    def _():
        own_far.wait_send()
        for b in range(count):
            for c in range(chunks):
                g_copy(b, c).wait_send()

    @pl.when(root)
    def _():
        for b in range(count):
            across_copy(b, xcol.at[b]).wait_send()
            pair_copy(b, xcol.at[b]).wait_send()
            hacross(b).wait_send()
            hpair(b).wait_send()

    @pl.when(relay)
    def _():
        for b in range(count):
            pair_copy(b, xw.at[b]).wait_send()
            hpair(b).wait_send()

    @pl.when(jnp.logical_not(root))
    def _():
        for b in range(count):
            h_copy(b).wait_send()


def fused(tokens, routes, shares, delta, bg, bu, bd, gl, gr, ul, ur, dl, dr):
    bf16, f32 = jnp.bfloat16, jnp.float32
    count = PLANE
    rows, feats = tokens.shape
    depth, cols = bg.shape
    exp_here, rank, _ = gr.shape
    span = exp_here * rank
    sets = -(-delta.shape[0] // 8) * 8
    chunks = cols // LANES if cols % LANES == 0 else 1
    sem = pltpu.SemaphoreType.DMA
    vm = pltpu.VMEM
    out_feats = bd.shape[1]
    top = routes.shape[1]
    hbm = pl.BlockSpec(memory_space=pl.ANY)
    four, three = sem((count,)), sem((3, count))
    grid4 = sem((count, chunks))
    return pl.pallas_call(
        kernel,
        out_shape=jax.ShapeDtypeStruct((rows, out_feats), bf16),
        in_specs=[hbm, hbm, hbm, pl.BlockSpec(memory_space=pltpu.SMEM)] + [hbm] * 9,
        out_specs=pl.BlockSpec(memory_space=pltpu.VMEM),
        scratch_shapes=[
            vm((top, rows), jnp.int32), vm((top, rows), f32),
            vm((depth, 2 * cols), bf16),
            vm((2 * span, feats), bf16),
            vm(bd.shape, bf16),
            vm((span, out_feats), bf16),
            vm((span, cols), bf16), vm((span, cols), bf16), vm((span, cols), bf16),
            vm((count, rows, feats), bf16),
            vm((count, rows, feats), bf16),
            vm((count, sets, rows), f32),
            vm((count, rows, 2 * cols), f32),
            vm((count, rows, 2 * cols), bf16),
            vm((count, rows, 2 * cols), bf16),
            vm((count, rows, 2 * cols), bf16),
            vm((count, rows, 2 * cols), bf16),
            vm((count, rows, 2 * cols), bf16),
            vm((count, rows, 2 * span), f32),
            vm((count, rows, 2 * span), bf16),
            vm((3, count, rows, 2 * span), bf16),
            vm((exp_here * rows, cols), bf16),
            vm((count, rows, cols), f32),
            vm((count, rows, cols), bf16),
            vm((count, count, rows, cols), bf16),
            vm((count, rows, cols), bf16),
            vm((count, rows, span), f32),
            vm((count, rows, span), bf16),
            vm((3, count, rows, span), bf16),
            vm((count, rows, out_feats), bf16),
            vm((count, rows, out_feats), bf16),
            vm((rows, out_feats), f32),
            sem((2,)), sem((3,)), four, four, four, sem((count, 2)), four,
            grid4, grid4, grid4, grid4, grid4, grid4, three, three,
            four, sem((count, count)), sem((2, count)), four, three, three, four, four, sem((10 + 2 * chunks,)),
        ],
        compiler_params=pltpu.CompilerParams(collective_id=0, has_side_effects=True, vmem_limit_bytes=60 * 1024 * 1024),
    )(
        tokens, routes.T, shares.T, delta, bg, bu, bd,
        jnp.swapaxes(gl, 1, 2).reshape(span, feats), gr.reshape(span, cols),
        jnp.swapaxes(ul, 1, 2).reshape(span, feats), ur.reshape(span, cols),
        jnp.swapaxes(dl, 1, 2).reshape(span, cols), dr.reshape(span, out_feats),
    )


def shards(
    tokens,
    routes,
    gate_weights,
    delta_of,
    base_gate,
    base_up,
    base_down,
    gate_left,
    gate_right,
    up_left,
    up_right,
    down_left,
    down_right,
):
    if lax.axis_size("narrow") == PLANE and lax.axis_size("wide") == PLANE:
        return fused(
            tokens, routes, gate_weights, delta_of, base_gate, base_up, base_down,
            gate_left, gate_right, up_left, up_right, down_left, down_right,
        )
    exp_here, _, rank = gate_left.shape
    experts = delta_of.shape[0]
    mine = lax.axis_index("wide")
    bf16 = jnp.bfloat16

    expert_ids = lax.broadcasted_iota(jnp.int32, (1, 1, experts), 2)
    named = routes[:, :, None] == expert_ids
    delta_ids = jnp.sum(jnp.where(named, delta_of[None, None, :], 0), axis=2)
    weight_of = jnp.sum(
        jnp.where(delta_ids[:, :, None] == expert_ids, gate_weights[:, :, None], 0.0), axis=1
    )
    weights = lax.all_gather(weight_of, "wide", axis=0, tiled=True)
    weights = lax.dynamic_slice_in_dim(weights, mine * exp_here, exp_here, axis=1)

    rows = lax.all_gather(tokens, "wide", axis=0, tiled=True)
    full = lax.all_gather(rows, "narrow", axis=1, tiled=True)
    depth = base_gate.shape[0]
    part = lax.dynamic_slice_in_dim(full, mine * depth, depth, axis=1)

    base_both = jnp.concatenate([base_gate, base_up], axis=1)
    both = lax.psum(dot32(part, base_both), "wide")
    columns = base_gate.shape[1]

    lefts = jnp.concatenate([gate_left, up_left], axis=0)
    low = lax.psum(jnp.einsum("td,edr->ter", rows, lefts, preferred_element_type=jnp.float32), "narrow")
    low = low.astype(bf16)

    mixed = 0.0
    thin = []
    for e in range(exp_here):
        gate = both[:, :columns] + dot32(low[:, e], gate_right[e])
        up = both[:, columns:] + dot32(low[:, exp_here + e], up_right[e])
        hidden = jax.nn.silu(gate) * up * weights[:, e : e + 1]
        mixed = mixed + hidden
        thin.append(dot32(hidden.astype(bf16), down_left[e]))
    mixed = lax.psum(mixed, "wide").astype(bf16)
    mixed_full = lax.all_gather(mixed, "narrow", axis=1, tiled=True)
    depth = base_down.shape[0]
    mixed_part = lax.dynamic_slice_in_dim(mixed_full, mine * depth, depth, axis=1)
    thin = lax.psum(jnp.concatenate(thin, axis=1), "narrow").astype(bf16)
    out = dot32(mixed_part, base_down) + dot32(thin, down_right.reshape(exp_here * rank, -1))
    out = lax.psum_scatter(out, "wide", scatter_dimension=0, tiled=True)
    return out.astype(bf16)


def solution(mesh):
    return jax.shard_map(
        shards,
        mesh=mesh,
        in_specs=(
            P(("groups", "wide"), "narrow"),
            P(("groups", "wide"), None),
            P(("groups", "wide"), None),
            P(),
            P("wide", "narrow"),
            P("wide", "narrow"),
            P("wide", "narrow"),
            P("wide", "narrow", None),
            P("wide", None, "narrow"),
            P("wide", "narrow", None),
            P("wide", None, "narrow"),
            P("wide", "narrow", None),
            P("wide", None, "narrow"),
        ),
        out_specs=P(("groups", "wide"), "narrow"),
        check_vma=False,
    )
```

```python
import jax
import jax.numpy as jnp
from jax import lax
from jax.experimental import pallas as pl
from jax.experimental.pallas import tpu as pltpu
from jax.sharding import PartitionSpec as P


def dot32(a, b):
    return jnp.dot(a, b, preferred_element_type=jnp.float32)


def dot32t(a, b):
    return lax.dot_general(a, b, (((1,), (1,)), ((), ())), preferred_element_type=jnp.float32)


PLANE = 4

LANES = 128


ORDER = (1, 2, 0, 3)


def kernel(
    tok, routes_hbm, shares_hbm, delta, bg_hbm, bu_hbm, bd_hbm, gl_hbm, gr_hbm, ul_hbm, ur_hbm, dl_hbm, dr_hbm, out,
    routes, shares, bgu, lefts, bd, dr, gr, ur, dl,
    xcol, xw, wts, gpart, gsend, grecv, gxs, gxr, gall, apart, asend, arecv,
    hst, hacc, hsend, hrecv, hpl, bpart, bsend, brecv, osend, orecv, oown,
    ti_s, to_s, tok_r, wt_s, wt_r, bs_s, bs_r, g_s, g_r, x_s, x_r, f_s, f_r, a_s, a_r,
    h_s, h_r, hb_s, hb_r, b_s, b_r, o_s, o_r, in_s,
):
    bf16, f32 = jnp.bfloat16, jnp.float32
    count = PLANE
    w, n = lax.axis_index("wide"), lax.axis_index("narrow")
    rows = tok.shape[0]
    span, cols = gr.shape
    exp_here = delta.shape[0] // count
    rank = span // exp_here
    chunk = LANES if cols % LANES == 0 else cols
    chunks = cols // chunk
    side = w // 2
    sign = 1 - 2 * side

    def mir(j):
        return j + side * (3 - 2 * j)

    depth = mir(w)
    inner = depth == 1
    end = depth == 0
    root = n == w
    relay = n == lax.rem(w + 2, count)
    pair = n + 1 - 2 * lax.rem(n, 2)
    across = lax.rem(n + 2, count)
    beside = (pair, across, lax.rem(pair + 2, count))
    inward = w + sign
    buddy = w + 1 - 2 * lax.rem(w, 2)

    def up_of(d):
        return lax.rem(w + d, count)

    pairs = [
        (tok, xcol.at[w]), (routes_hbm, routes), (shares_hbm, shares),
    ]
    pairs += [(gl_hbm, lefts.at[pl.ds(0, span)]), (ul_hbm, lefts.at[pl.ds(span, span)])]
    first = len(pairs)
    for c in range(chunks):
        for k, base in enumerate((bg_hbm, bu_hbm)):
            pairs.append((base.at[:, pl.ds(c * chunk, chunk)], bgu.at[:, pl.ds((2 * c + k) * chunk, chunk)]))
    second = len(pairs)
    pairs += [(gr_hbm, gr), (ur_hbm, ur), (dl_hbm, dl)]
    third = len(pairs)
    pairs += [(bd_hbm, bd), (dr_hbm, dr)]
    loads = [pltpu.make_async_copy(a, b, in_s.at[i]) for i, (a, b) in enumerate(pairs)]

    def copy(src, dst, ss, rs, axis, peer):
        return pltpu.make_async_remote_copy(
            src_ref=src, dst_ref=dst, send_sem=ss, recv_sem=rs,
            device_id={axis: peer}, device_id_type=pl.DeviceIdType.MESH,
        )

    barrier = pltpu.get_barrier_semaphore()
    for d in range(1, count):
        pl.semaphore_signal(barrier, inc=1, device_id={"wide": up_of(d)}, device_id_type=pl.DeviceIdType.MESH)
    for peer in beside:
        pl.semaphore_signal(barrier, inc=1, device_id={"narrow": peer}, device_id_type=pl.DeviceIdType.MESH)
    for load in loads:
        load.start()
    pl.semaphore_wait(barrier, 2 * (count - 1))

    own_in = copy(tok, xcol.at[w], ti_s.at[0], tok_r.at[w], "wide", inward)
    own_out = copy(tok, xcol.at[w], to_s.at[0], tok_r.at[w], "wide", buddy)

    own_far = copy(tok, xcol.at[w], ti_s.at[1], tok_r.at[w], "wide", count - 1 - buddy)

    def tok_in(b):
        return copy(xcol.at[b], xcol.at[b], ti_s.at[1], tok_r.at[b], "wide", buddy)

    def tok_out(b, k):
        return copy(xcol.at[b], xcol.at[b], to_s.at[k], tok_r.at[b], "wide", buddy)

    def pair_copy(b, src):
        return copy(src, xw.at[b], bs_s.at[b, 0], bs_r.at[b], "narrow", pair)

    def across_copy(b, src):
        return copy(src, xw.at[b], bs_s.at[b, 1], bs_r.at[b], "narrow", across)

    def wt_copy(d):
        return copy(wts.at[w], wts.at[w], wt_s.at[d], wt_r.at[w], "wide", up_of(d))

    def wt_from(d):
        return copy(wts.at[up_of(d)], wts.at[up_of(d)], wt_s.at[d], wt_r.at[up_of(d)], "wide", up_of(d))

    own_in.start()

    @pl.when(end)
    def _():
        own_far.start()

    @pl.when(inner)
    def _():
        own_out.start()

    @pl.when(root)
    def _():
        across_copy(w, tok).start()
        pair_copy(w, tok).start()

    for load in loads[:3]:
        load.wait()
    named, ids = routes[...], jnp.zeros(routes.shape, jnp.int32)
    for e in range(delta.shape[0]):
        ids = jnp.where(named == e, delta[e], ids)
    sets = lax.broadcasted_iota(jnp.int32, wts.shape[1:], 0)
    table = jnp.zeros(sets.shape, f32)
    for k in range(routes.shape[0]):
        table = table + jnp.where(sets == ids[k : k + 1], shares[k : k + 1, :], 0.0)
    wts[w] = table

    @pl.when(root)
    def _():
        xw[w] = xcol[w]

    def a_copy(k, b):
        return copy(asend.at[b], arecv.at[k, b], a_s.at[k, b], a_r.at[k, b], "narrow", beside[k])

    def low(j):
        b = w if j == 0 else (mir(1 - depth) if j == 1 else mir(j))
        if j > 0:

            @pl.when(jnp.logical_and(end, jnp.logical_not(root)))
            def _():
                tok_in(b).wait_recv()

        thin = dot32t(xcol[b], lefts[...])
        apart[b] = thin
        asend[b] = thin.astype(bf16)
        for k in range(3):
            a_copy(k, b).start()

    for load in loads[3:first]:
        load.wait()
    low(0)
    for load in loads[first:second]:
        load.wait()

    def part_of(c):
        return pl.ds(2 * c * chunk, 2 * chunk)

    def g_copy(b, c):
        return copy(gsend.at[b, :, part_of(c)], grecv.at[b, :, part_of(c)], g_s.at[b, c], g_r.at[b, c], "wide", buddy)

    def x_copy(b, c):
        return copy(gxs.at[b, :, part_of(c)], gxr.at[b, :, part_of(c)], x_s.at[b, c], x_r.at[b, c], "wide", inward)

    def f_copy(b, c):
        return copy(gall.at[b, :, part_of(c)], gall.at[b, :, part_of(c)], f_s.at[b, c], f_r.at[b, c], "wide", buddy)

    def arrive(j, who):
        b = mir(1 - depth) if j == 1 else mir(j)

        @pl.when(jnp.logical_and(who, jnp.logical_or(root, inner)))
        def _():
            tok_in(b).wait_recv()

        if j > 1 and who is inner:

            @pl.when(inner)
            def _():
                tok_out(b, j - 1).start()

        @pl.when(jnp.logical_and(who, root))
        def _():
            across_copy(b, xcol.at[b]).start()
            pair_copy(b, xcol.at[b]).start()
            xw[b] = xcol[b]

    def base(j):
        b = w if j == 0 else (mir(1 - depth) if j == 1 else mir(j))

        @pl.when(jnp.logical_not(root))
        def _():
            pair_copy(b, xw.at[b]).wait_recv()

        @pl.when(relay)
        def _():
            pair_copy(b, xw.at[b]).start()

        both = dot32(xw[b], bgu[...])
        gpart[b] = both

        @pl.when(end)
        def _():
            gsend[b] = both.astype(bf16)
            for c in range(chunks):
                g_copy(b, c).start()

    def side_sum(j):
        b = mir(j)

        @pl.when(inner)
        def _():
            for c in range(chunks):
                part = slice(2 * c * chunk, 2 * (c + 1) * chunk)
                g_copy(b, c).wait_recv()
                total = gpart[b, :, part] + grecv[b, :, part].astype(f32)
                gpart[b, :, part] = total
                gxs[b, :, part] = total.astype(bf16)
                x_copy(b, c).start()

    base(0)
    for j in (1, 2, 3):
        arrive(j, inner)
    for j in (1, 2, 3):
        arrive(j, end)
        base(j)
    for d in range(1, count):
        wt_copy(d).start()
    side_sum(0)
    side_sum(1)
    low(1)
    low(2)
    low(3)
    side_sum(2)
    side_sum(3)
    for load in loads[second:]:
        load.wait()
    for d in range(1, count):
        wt_from(d).wait_recv()

    def settle(b):
        @pl.when(inner)
        def _():
            for c in range(chunks):
                part = slice(2 * c * chunk, 2 * (c + 1) * chunk)
                x_copy(b, c).wait_recv()
                total = gpart[b, :, part] + gxr[b, :, part].astype(f32)
                gpart[b, :, part] = total
                gall[b, :, part] = total.astype(bf16)
                f_copy(b, c).start()

    def fetch(b):
        @pl.when(end)
        def _():
            for c in range(chunks):
                part = slice(2 * c * chunk, 2 * (c + 1) * chunk)
                f_copy(b, c).wait_recv()
                gpart[b, :, part] = gall[b, :, part].astype(f32)

    groups_of = lax.broadcasted_iota(jnp.int32, (rows, span), 1) // rank

    def spread(block):
        return jnp.concatenate(
            [jnp.where(groups_of == e, block, jnp.zeros_like(block)) for e in range(exp_here)], axis=0
        )

    def b_copy(k, b):
        return copy(bsend.at[b], brecv.at[k, b], b_s.at[k, b], b_r.at[k, b], "narrow", beside[k])

    def hidden_of(b):
        scales = wts[b].T
        ids = lax.broadcasted_iota(jnp.int32, scales.shape, 1)
        scale = [
            jnp.sum(jnp.where(ids == w * exp_here + e, scales, 0.0), axis=1, keepdims=True) for e in range(exp_here)
        ]
        low_sum = apart[b]
        for k in range(3):
            a_copy(k, b).wait_recv()
            low_sum = low_sum + arecv[k, b].astype(f32)
        low_sum = low_sum.astype(bf16)
        thin_gate, thin_up = spread(low_sum[:, :span]), spread(low_sum[:, span:])
        for c in range(chunks):
            part = slice(c * chunk, (c + 1) * chunk)
            gates = gpart[b, :, 2 * c * chunk : (2 * c + 1) * chunk]
            ups = gpart[b, :, (2 * c + 1) * chunk : 2 * (c + 1) * chunk]
            more_gate, more_up = dot32(thin_gate, gr[:, part]), dot32(thin_up, ur[:, part])
            acc = None
            for e in range(exp_here):
                own = slice(e * rows, (e + 1) * rows)
                gate, up = gates + more_gate[own], ups + more_up[own]
                hidden = gate / (1.0 + jnp.exp(-gate)) * up * scale[e]
                acc = hidden if acc is None else acc + hidden
                hst[own, part] = hidden.astype(bf16)
            hacc[b, :, part] = acc
        thin = dot32t(hst[...], dl[...])
        mixed = jnp.zeros((rows, span), f32)
        for e in range(exp_here):
            mixed = mixed + jnp.where(groups_of == e, thin[e * rows : (e + 1) * rows], 0.0)
        bpart[b] = mixed
        bsend[b] = mixed.astype(bf16)
        for k in range(3):
            b_copy(k, b).start()

    def h_copy(b):
        return copy(hsend.at[b], hrecv.at[w, b], h_s.at[b], h_r.at[w, b], "wide", n)

    def h_from(k, b):
        return copy(hsend.at[b], hrecv.at[k, b], h_s.at[b], h_r.at[k, b], "wide", k)

    def pass_on(b):
        @pl.when(jnp.logical_not(root))
        def _():
            hsend[b] = hacc[b].astype(bf16)
            h_copy(b).start()

    def hpair(b):
        return copy(hpl.at[b], hpl.at[b], hb_s.at[0, b], hb_r.at[b], "narrow", pair)

    def hacross(b):
        return copy(hpl.at[b], hpl.at[b], hb_s.at[1, b], hb_r.at[b], "narrow", across)

    def collect(b):
        @pl.when(root)
        def _():
            whole = hacc[b]
            for d in range(1, count):
                h_from(up_of(d), b).wait_recv()
                whole = whole + hrecv[up_of(d), b].astype(f32)
            hpl[b] = whole.astype(bf16)
            hacross(b).start()
            hpair(b).start()

    def o_copy(b):
        return copy(osend.at[b], orecv.at[w], o_s.at[b], o_r.at[w], "wide", b)

    def o_from(k):
        return copy(osend.at[k], orecv.at[k], o_s.at[k], o_r.at[k], "wide", k)

    def project(b):
        @pl.when(jnp.logical_not(root))
        def _():
            hpair(b).wait_recv()

        @pl.when(relay)
        def _():
            hpair(b).start()

        thin = bpart[b]
        for k in range(3):
            b_copy(k, b).wait_recv()
            thin = thin + brecv[k, b].astype(f32)
        part = dot32(hpl[b], bd[...]) + dot32(thin.astype(bf16), dr[...])

        @pl.when(w == b)
        def _():
            oown[...] = part

        @pl.when(w != b)
        def _():
            osend[b] = part.astype(bf16)
            o_copy(b).start()

    for b in ORDER:
        settle(b)
    for i in range(count):
        fetch(ORDER[i])
        hidden_of(ORDER[i])
        pass_on(ORDER[i])
    for b in ORDER:
        collect(b)
        project(b)
    total = oown[...]
    for d in range(1, count):
        k = up_of(d)
        o_from(k).wait_recv()
        total = total + orecv[k].astype(f32)
    out[...] = total.astype(bf16)

    own_in.wait_send()
    for d in range(1, count):
        wt_copy(d).wait_send()
        o_from(up_of(d)).wait_send()
    for k in range(3):
        for b in range(count):
            a_copy(k, b).wait_send()
            b_copy(k, b).wait_send()

    @pl.when(inner)
    def _():
        own_out.wait_send()
        for j in (2, 3):
            tok_out(mir(j), j - 1).wait_send()
        for b in range(count):
            for c in range(chunks):
                x_copy(b, c).wait_send()
                f_copy(b, c).wait_send()

    @pl.when(end)
    def _():
        own_far.wait_send()
        for b in range(count):
            for c in range(chunks):
                g_copy(b, c).wait_send()

    @pl.when(root)
    def _():
        for b in range(count):
            across_copy(b, xcol.at[b]).wait_send()
            pair_copy(b, xcol.at[b]).wait_send()
            hacross(b).wait_send()
            hpair(b).wait_send()

    @pl.when(relay)
    def _():
        for b in range(count):
            pair_copy(b, xw.at[b]).wait_send()
            hpair(b).wait_send()

    @pl.when(jnp.logical_not(root))
    def _():
        for b in range(count):
            h_copy(b).wait_send()


def fused(tokens, routes, shares, delta, bg, bu, bd, gl, gr, ul, ur, dl, dr):
    bf16, f32 = jnp.bfloat16, jnp.float32
    count = PLANE
    rows, feats = tokens.shape
    depth, cols = bg.shape
    exp_here, rank, _ = gr.shape
    span = exp_here * rank
    sets = -(-delta.shape[0] // 8) * 8
    chunks = cols // LANES if cols % LANES == 0 else 1
    sem = pltpu.SemaphoreType.DMA
    vm = pltpu.VMEM
    out_feats = bd.shape[1]
    top = routes.shape[1]
    hbm = pl.BlockSpec(memory_space=pl.ANY)
    four, three = sem((count,)), sem((3, count))
    grid4 = sem((count, chunks))
    return pl.pallas_call(
        kernel,
        out_shape=jax.ShapeDtypeStruct((rows, out_feats), bf16),
        in_specs=[hbm, hbm, hbm, pl.BlockSpec(memory_space=pltpu.SMEM)] + [hbm] * 9,
        out_specs=pl.BlockSpec(memory_space=pltpu.VMEM),
        scratch_shapes=[
            vm((top, rows), jnp.int32), vm((top, rows), f32),
            vm((depth, 2 * cols), bf16),
            vm((2 * span, feats), bf16),
            vm(bd.shape, bf16),
            vm((span, out_feats), bf16),
            vm((span, cols), bf16), vm((span, cols), bf16), vm((span, cols), bf16),
            vm((count, rows, feats), bf16),
            vm((count, rows, feats), bf16),
            vm((count, sets, rows), f32),
            vm((count, rows, 2 * cols), f32),
            vm((count, rows, 2 * cols), bf16),
            vm((count, rows, 2 * cols), bf16),
            vm((count, rows, 2 * cols), bf16),
            vm((count, rows, 2 * cols), bf16),
            vm((count, rows, 2 * cols), bf16),
            vm((count, rows, 2 * span), f32),
            vm((count, rows, 2 * span), bf16),
            vm((3, count, rows, 2 * span), bf16),
            vm((exp_here * rows, cols), bf16),
            vm((count, rows, cols), f32),
            vm((count, rows, cols), bf16),
            vm((count, count, rows, cols), bf16),
            vm((count, rows, cols), bf16),
            vm((count, rows, span), f32),
            vm((count, rows, span), bf16),
            vm((3, count, rows, span), bf16),
            vm((count, rows, out_feats), bf16),
            vm((count, rows, out_feats), bf16),
            vm((rows, out_feats), f32),
            sem((2,)), sem((3,)), four, four, four, sem((count, 2)), four,
            grid4, grid4, grid4, grid4, grid4, grid4, three, three,
            four, sem((count, count)), sem((2, count)), four, three, three, four, four, sem((10 + 2 * chunks,)),
        ],
        compiler_params=pltpu.CompilerParams(collective_id=0, has_side_effects=True, vmem_limit_bytes=60 * 1024 * 1024),
    )(
        tokens, routes.T, shares.T, delta, bg, bu, bd,
        jnp.swapaxes(gl, 1, 2).reshape(span, feats), gr.reshape(span, cols),
        jnp.swapaxes(ul, 1, 2).reshape(span, feats), ur.reshape(span, cols),
        jnp.swapaxes(dl, 1, 2).reshape(span, cols), dr.reshape(span, out_feats),
    )


def shards(
    tokens,
    routes,
    gate_weights,
    delta_of,
    base_gate,
    base_up,
    base_down,
    gate_left,
    gate_right,
    up_left,
    up_right,
    down_left,
    down_right,
):
    if lax.axis_size("narrow") == PLANE and lax.axis_size("wide") == PLANE:
        return fused(
            tokens, routes, gate_weights, delta_of, base_gate, base_up, base_down,
            gate_left, gate_right, up_left, up_right, down_left, down_right,
        )
    exp_here, _, rank = gate_left.shape
    experts = delta_of.shape[0]
    mine = lax.axis_index("wide")
    bf16 = jnp.bfloat16

    expert_ids = lax.broadcasted_iota(jnp.int32, (1, 1, experts), 2)
    named = routes[:, :, None] == expert_ids
    delta_ids = jnp.sum(jnp.where(named, delta_of[None, None, :], 0), axis=2)
    weight_of = jnp.sum(
        jnp.where(delta_ids[:, :, None] == expert_ids, gate_weights[:, :, None], 0.0), axis=1
    )
    weights = lax.all_gather(weight_of, "wide", axis=0, tiled=True)
    weights = lax.dynamic_slice_in_dim(weights, mine * exp_here, exp_here, axis=1)

    rows = lax.all_gather(tokens, "wide", axis=0, tiled=True)
    full = lax.all_gather(rows, "narrow", axis=1, tiled=True)
    depth = base_gate.shape[0]
    part = lax.dynamic_slice_in_dim(full, mine * depth, depth, axis=1)

    base_both = jnp.concatenate([base_gate, base_up], axis=1)
    both = lax.psum(dot32(part, base_both), "wide")
    columns = base_gate.shape[1]

    lefts = jnp.concatenate([gate_left, up_left], axis=0)
    low = lax.psum(jnp.einsum("td,edr->ter", rows, lefts, preferred_element_type=jnp.float32), "narrow")
    low = low.astype(bf16)

    mixed = 0.0
    thin = []
    for e in range(exp_here):
        gate = both[:, :columns] + dot32(low[:, e], gate_right[e])
        up = both[:, columns:] + dot32(low[:, exp_here + e], up_right[e])
        hidden = jax.nn.silu(gate) * up * weights[:, e : e + 1]
        mixed = mixed + hidden
        thin.append(dot32(hidden.astype(bf16), down_left[e]))
    mixed = lax.psum(mixed, "wide").astype(bf16)
    mixed_full = lax.all_gather(mixed, "narrow", axis=1, tiled=True)
    depth = base_down.shape[0]
    mixed_part = lax.dynamic_slice_in_dim(mixed_full, mine * depth, depth, axis=1)
    thin = lax.psum(jnp.concatenate(thin, axis=1), "narrow").astype(bf16)
    out = dot32(mixed_part, base_down) + dot32(thin, down_right.reshape(exp_here * rank, -1))
    out = lax.psum_scatter(out, "wide", scatter_dimension=0, tiled=True)
    return out.astype(bf16)


def solution(mesh):
    return jax.shard_map(
        shards,
        mesh=mesh,
        in_specs=(
            P(("groups", "wide"), "narrow"),
            P(("groups", "wide"), None),
            P(("groups", "wide"), None),
            P(),
            P("wide", "narrow"),
            P("wide", "narrow"),
            P("wide", "narrow"),
            P("wide", "narrow", None),
            P("wide", None, "narrow"),
            P("wide", "narrow", None),
            P("wide", None, "narrow"),
            P("wide", "narrow", None),
            P("wide", None, "narrow"),
        ),
        out_specs=P(("groups", "wide"), "narrow"),
        check_vma=False,
    )
```

```python
import jax
import jax.numpy as jnp
from jax import lax
from jax.experimental import pallas as pl
from jax.experimental.pallas import tpu as pltpu
from jax.sharding import PartitionSpec as P


def dot32(a, b):
    return jnp.dot(a, b, preferred_element_type=jnp.float32)


def dot32t(a, b):
    return lax.dot_general(a, b, (((1,), (1,)), ((), ())), preferred_element_type=jnp.float32)


PLANE = 4

LANES = 128


ORDER = (1, 2, 0, 3)


def kernel(
    tok, routes_hbm, shares_hbm, delta, bg_hbm, bu_hbm, bd_hbm, gl_hbm, gr_hbm, ul_hbm, ur_hbm, dl_hbm, dr_hbm, out,
    routes, shares, bgu, lefts, bd, dr, gr, ur, dl,
    xcol, xw, wts, gpart, gsend, grecv, gxs, gxr, gall, apart, asend, arecv,
    hst, hacc, hsend, hrecv, hpl, bpart, bsend, brecv, osend, orecv, oown,
    ti_s, to_s, tok_r, wt_s, wt_r, bs_s, bs_r, g_s, g_r, x_s, x_r, f_s, f_r, a_s, a_r,
    h_s, h_r, hb_s, hb_r, b_s, b_r, o_s, o_r, in_s,
):
    bf16, f32 = jnp.bfloat16, jnp.float32
    count = PLANE
    w, n = lax.axis_index("wide"), lax.axis_index("narrow")
    rows = tok.shape[0]
    span, cols = gr.shape
    exp_here = delta.shape[0] // count
    rank = span // exp_here
    chunk = LANES if cols % LANES == 0 else cols
    chunks = cols // chunk
    side = w // 2
    sign = 1 - 2 * side

    def mir(j):
        return j + side * (3 - 2 * j)

    depth = mir(w)
    inner = depth == 1
    end = depth == 0
    root = n == w
    relay = n == lax.rem(w + 2, count)
    pair = n + 1 - 2 * lax.rem(n, 2)
    across = lax.rem(n + 2, count)
    beside = (pair, across, lax.rem(pair + 2, count))
    inward = w + sign
    buddy = w + 1 - 2 * lax.rem(w, 2)

    def up_of(d):
        return lax.rem(w + d, count)

    pairs = [
        (tok, xcol.at[w]), (routes_hbm, routes), (shares_hbm, shares),
    ]
    pairs += [(gl_hbm, lefts.at[pl.ds(0, span)]), (ul_hbm, lefts.at[pl.ds(span, span)])]
    first = len(pairs)
    for c in range(chunks):
        for k, base in enumerate((bg_hbm, bu_hbm)):
            pairs.append((base.at[:, pl.ds(c * chunk, chunk)], bgu.at[:, pl.ds((2 * c + k) * chunk, chunk)]))
    second = len(pairs)
    pairs += [(gr_hbm, gr), (ur_hbm, ur), (dl_hbm, dl)]
    third = len(pairs)
    pairs += [(bd_hbm, bd), (dr_hbm, dr)]
    loads = [pltpu.make_async_copy(a, b, in_s.at[i]) for i, (a, b) in enumerate(pairs)]

    def copy(src, dst, ss, rs, axis, peer):
        return pltpu.make_async_remote_copy(
            src_ref=src, dst_ref=dst, send_sem=ss, recv_sem=rs,
            device_id={axis: peer}, device_id_type=pl.DeviceIdType.MESH,
        )

    barrier = pltpu.get_barrier_semaphore()
    for d in range(1, count):
        pl.semaphore_signal(barrier, inc=1, device_id={"wide": up_of(d)}, device_id_type=pl.DeviceIdType.MESH)
    for peer in beside:
        pl.semaphore_signal(barrier, inc=1, device_id={"narrow": peer}, device_id_type=pl.DeviceIdType.MESH)
    for load in loads:
        load.start()
    pl.semaphore_wait(barrier, 2 * (count - 1))

    own_in = copy(tok, xcol.at[w], ti_s.at[0], tok_r.at[w], "wide", inward)
    own_out = copy(tok, xcol.at[w], to_s.at[0], tok_r.at[w], "wide", buddy)

    own_far = copy(tok, xcol.at[w], ti_s.at[1], tok_r.at[w], "wide", count - 1 - buddy)

    def tok_in(b):
        return copy(xcol.at[b], xcol.at[b], ti_s.at[1], tok_r.at[b], "wide", buddy)

    def tok_out(b, k):
        return copy(xcol.at[b], xcol.at[b], to_s.at[k], tok_r.at[b], "wide", buddy)

    def pair_copy(b, src):
        return copy(src, xw.at[b], bs_s.at[b, 0], bs_r.at[b], "narrow", pair)

    def across_copy(b, src):
        return copy(src, xw.at[b], bs_s.at[b, 1], bs_r.at[b], "narrow", across)

    def wt_copy(d):
        return copy(wts.at[w], wts.at[w], wt_s.at[d], wt_r.at[w], "wide", up_of(d))

    def wt_from(d):
        return copy(wts.at[up_of(d)], wts.at[up_of(d)], wt_s.at[d], wt_r.at[up_of(d)], "wide", up_of(d))

    own_in.start()

    @pl.when(end)
    def _():
        own_far.start()

    @pl.when(inner)
    def _():
        own_out.start()

    @pl.when(root)
    def _():
        across_copy(w, tok).start()
        pair_copy(w, tok).start()

    for load in loads[:3]:
        load.wait()
    named, ids = routes[...], jnp.zeros(routes.shape, jnp.int32)
    for e in range(delta.shape[0]):
        ids = jnp.where(named == e, delta[e], ids)
    sets = lax.broadcasted_iota(jnp.int32, wts.shape[1:], 0)
    table = jnp.zeros(sets.shape, f32)
    for k in range(routes.shape[0]):
        table = table + jnp.where(sets == ids[k : k + 1], shares[k : k + 1, :], 0.0)
    wts[w] = table
    for d in range(1, count):
        wt_copy(d).start()

    @pl.when(root)
    def _():
        xw[w] = xcol[w]

    def a_copy(k, b):
        return copy(asend.at[b], arecv.at[k, b], a_s.at[k, b], a_r.at[k, b], "narrow", beside[k])

    def low(j):
        b = w if j == 0 else (mir(1 - depth) if j == 1 else mir(j))
        if j > 0:

            @pl.when(jnp.logical_and(end, jnp.logical_not(root)))
            def _():
                tok_in(b).wait_recv()

        thin = dot32t(xcol[b], lefts[...])
        apart[b] = thin
        asend[b] = thin.astype(bf16)
        for k in range(3):
            a_copy(k, b).start()

    for load in loads[3:first]:
        load.wait()
    low(0)
    for load in loads[first:second]:
        load.wait()

    def part_of(c):
        return pl.ds(2 * c * chunk, 2 * chunk)

    def g_copy(b, c):
        return copy(gsend.at[b, :, part_of(c)], grecv.at[b, :, part_of(c)], g_s.at[b, c], g_r.at[b, c], "wide", buddy)

    def x_copy(b, c):
        return copy(gxs.at[b, :, part_of(c)], gxr.at[b, :, part_of(c)], x_s.at[b, c], x_r.at[b, c], "wide", inward)

    def f_copy(b, c):
        return copy(gall.at[b, :, part_of(c)], gall.at[b, :, part_of(c)], f_s.at[b, c], f_r.at[b, c], "wide", buddy)

    def arrive(j, who):
        b = mir(1 - depth) if j == 1 else mir(j)

        @pl.when(jnp.logical_and(who, jnp.logical_or(root, inner)))
        def _():
            tok_in(b).wait_recv()

        if j > 1 and who is inner:

            @pl.when(inner)
            def _():
                tok_out(b, j - 1).start()

        @pl.when(jnp.logical_and(who, root))
        def _():
            across_copy(b, xcol.at[b]).start()
            pair_copy(b, xcol.at[b]).start()
            xw[b] = xcol[b]

    def base(j):
        b = w if j == 0 else (mir(1 - depth) if j == 1 else mir(j))

        @pl.when(jnp.logical_not(root))
        def _():
            pair_copy(b, xw.at[b]).wait_recv()

        @pl.when(relay)
        def _():
            pair_copy(b, xw.at[b]).start()

        both = dot32(xw[b], bgu[...])
        gpart[b] = both

        @pl.when(end)
        def _():
            gsend[b] = both.astype(bf16)
            for c in range(chunks):
                g_copy(b, c).start()

    def side_sum(j):
        b = mir(j)

        @pl.when(inner)
        def _():
            for c in range(chunks):
                part = slice(2 * c * chunk, 2 * (c + 1) * chunk)
                g_copy(b, c).wait_recv()
                total = gpart[b, :, part] + grecv[b, :, part].astype(f32)
                gpart[b, :, part] = total
                gxs[b, :, part] = total.astype(bf16)
                x_copy(b, c).start()

    base(0)
    for j in (1, 2, 3):
        arrive(j, inner)
    for j in (1, 2, 3):
        arrive(j, end)
        base(j)
    side_sum(0)
    side_sum(1)
    low(1)
    low(2)
    low(3)
    side_sum(2)
    side_sum(3)
    for load in loads[second:]:
        load.wait()
    for d in range(1, count):
        wt_from(d).wait_recv()

    def settle(b):
        @pl.when(inner)
        def _():
            for c in range(chunks):
                part = slice(2 * c * chunk, 2 * (c + 1) * chunk)
                x_copy(b, c).wait_recv()
                total = gpart[b, :, part] + gxr[b, :, part].astype(f32)
                gpart[b, :, part] = total
                gall[b, :, part] = total.astype(bf16)
                f_copy(b, c).start()

    def fetch(b):
        @pl.when(end)
        def _():
            for c in range(chunks):
                part = slice(2 * c * chunk, 2 * (c + 1) * chunk)
                f_copy(b, c).wait_recv()
                gpart[b, :, part] = gall[b, :, part].astype(f32)

    groups_of = lax.broadcasted_iota(jnp.int32, (rows, span), 1) // rank

    def spread(block):
        return jnp.concatenate(
            [jnp.where(groups_of == e, block, jnp.zeros_like(block)) for e in range(exp_here)], axis=0
        )

    def b_copy(k, b):
        return copy(bsend.at[b], brecv.at[k, b], b_s.at[k, b], b_r.at[k, b], "narrow", beside[k])

    def hidden_of(b):
        scales = wts[b].T
        ids = lax.broadcasted_iota(jnp.int32, scales.shape, 1)
        scale = [
            jnp.sum(jnp.where(ids == w * exp_here + e, scales, 0.0), axis=1, keepdims=True) for e in range(exp_here)
        ]
        low_sum = apart[b]
        for k in range(3):
            a_copy(k, b).wait_recv()
            low_sum = low_sum + arecv[k, b].astype(f32)
        low_sum = low_sum.astype(bf16)
        thin_gate, thin_up = spread(low_sum[:, :span]), spread(low_sum[:, span:])
        for c in range(chunks):
            part = slice(c * chunk, (c + 1) * chunk)
            gates = gpart[b, :, 2 * c * chunk : (2 * c + 1) * chunk]
            ups = gpart[b, :, (2 * c + 1) * chunk : 2 * (c + 1) * chunk]
            more_gate, more_up = dot32(thin_gate, gr[:, part]), dot32(thin_up, ur[:, part])
            acc = None
            for e in range(exp_here):
                own = slice(e * rows, (e + 1) * rows)
                gate, up = gates + more_gate[own], ups + more_up[own]
                hidden = gate / (1.0 + jnp.exp(-gate)) * up * scale[e]
                acc = hidden if acc is None else acc + hidden
                hst[own, part] = hidden.astype(bf16)
            hacc[b, :, part] = acc
        thin = dot32t(hst[...], dl[...])
        mixed = jnp.zeros((rows, span), f32)
        for e in range(exp_here):
            mixed = mixed + jnp.where(groups_of == e, thin[e * rows : (e + 1) * rows], 0.0)
        bpart[b] = mixed
        bsend[b] = mixed.astype(bf16)
        for k in range(3):
            b_copy(k, b).start()

    def h_copy(b):
        return copy(hsend.at[b], hrecv.at[w, b], h_s.at[b], h_r.at[w, b], "wide", n)

    def h_from(k, b):
        return copy(hsend.at[b], hrecv.at[k, b], h_s.at[b], h_r.at[k, b], "wide", k)

    def pass_on(b):
        @pl.when(jnp.logical_not(root))
        def _():
            hsend[b] = hacc[b].astype(bf16)
            h_copy(b).start()

    def hpair(b):
        return copy(hpl.at[b], hpl.at[b], hb_s.at[0, b], hb_r.at[b], "narrow", pair)

    def hacross(b):
        return copy(hpl.at[b], hpl.at[b], hb_s.at[1, b], hb_r.at[b], "narrow", across)

    def collect(b):
        @pl.when(root)
        def _():
            whole = hacc[b]
            for d in range(1, count):
                h_from(up_of(d), b).wait_recv()
                whole = whole + hrecv[up_of(d), b].astype(f32)
            hpl[b] = whole.astype(bf16)
            hacross(b).start()
            hpair(b).start()

    def o_copy(b):
        return copy(osend.at[b], orecv.at[w], o_s.at[b], o_r.at[w], "wide", b)

    def o_from(k):
        return copy(osend.at[k], orecv.at[k], o_s.at[k], o_r.at[k], "wide", k)

    def project(b):
        @pl.when(jnp.logical_not(root))
        def _():
            hpair(b).wait_recv()

        @pl.when(relay)
        def _():
            hpair(b).start()

        thin = bpart[b]
        for k in range(3):
            b_copy(k, b).wait_recv()
            thin = thin + brecv[k, b].astype(f32)
        part = dot32(hpl[b], bd[...]) + dot32(thin.astype(bf16), dr[...])

        @pl.when(w == b)
        def _():
            oown[...] = part

        @pl.when(w != b)
        def _():
            osend[b] = part.astype(bf16)
            o_copy(b).start()

    for b in ORDER:
        settle(b)
    for i in range(count):
        fetch(ORDER[i])
        hidden_of(ORDER[i])
        pass_on(ORDER[i])
    for b in ORDER:
        collect(b)
        project(b)
    total = oown[...]
    for d in range(1, count):
        k = up_of(d)
        o_from(k).wait_recv()
        total = total + orecv[k].astype(f32)
    out[...] = total.astype(bf16)

    own_in.wait_send()
    for d in range(1, count):
        wt_copy(d).wait_send()
        o_from(up_of(d)).wait_send()
    for k in range(3):
        for b in range(count):
            a_copy(k, b).wait_send()
            b_copy(k, b).wait_send()

    @pl.when(inner)
    def _():
        own_out.wait_send()
        for j in (2, 3):
            tok_out(mir(j), j - 1).wait_send()
        for b in range(count):
            for c in range(chunks):
                x_copy(b, c).wait_send()
                f_copy(b, c).wait_send()

    @pl.when(end)
    def _():
        own_far.wait_send()
        for b in range(count):
            for c in range(chunks):
                g_copy(b, c).wait_send()

    @pl.when(root)
    def _():
        for b in range(count):
            across_copy(b, xcol.at[b]).wait_send()
            pair_copy(b, xcol.at[b]).wait_send()
            hacross(b).wait_send()
            hpair(b).wait_send()

    @pl.when(relay)
    def _():
        for b in range(count):
            pair_copy(b, xw.at[b]).wait_send()
            hpair(b).wait_send()

    @pl.when(jnp.logical_not(root))
    def _():
        for b in range(count):
            h_copy(b).wait_send()


def fused(tokens, routes, shares, delta, bg, bu, bd, gl, gr, ul, ur, dl, dr):
    bf16, f32 = jnp.bfloat16, jnp.float32
    count = PLANE
    rows, feats = tokens.shape
    depth, cols = bg.shape
    exp_here, rank, _ = gr.shape
    span = exp_here * rank
    sets = -(-delta.shape[0] // 8) * 8
    chunks = cols // LANES if cols % LANES == 0 else 1
    sem = pltpu.SemaphoreType.DMA
    vm = pltpu.VMEM
    out_feats = bd.shape[1]
    top = routes.shape[1]
    hbm = pl.BlockSpec(memory_space=pl.ANY)
    four, three = sem((count,)), sem((3, count))
    grid4 = sem((count, chunks))
    return pl.pallas_call(
        kernel,
        out_shape=jax.ShapeDtypeStruct((rows, out_feats), bf16),
        in_specs=[hbm, hbm, hbm, pl.BlockSpec(memory_space=pltpu.SMEM)] + [hbm] * 9,
        out_specs=pl.BlockSpec(memory_space=pltpu.VMEM),
        scratch_shapes=[
            vm((top, rows), jnp.int32), vm((top, rows), f32),
            vm((depth, 2 * cols), bf16),
            vm((2 * span, feats), bf16),
            vm(bd.shape, bf16),
            vm((span, out_feats), bf16),
            vm((span, cols), bf16), vm((span, cols), bf16), vm((span, cols), bf16),
            vm((count, rows, feats), bf16),
            vm((count, rows, feats), bf16),
            vm((count, sets, rows), f32),
            vm((count, rows, 2 * cols), f32),
            vm((count, rows, 2 * cols), bf16),
            vm((count, rows, 2 * cols), bf16),
            vm((count, rows, 2 * cols), bf16),
            vm((count, rows, 2 * cols), bf16),
            vm((count, rows, 2 * cols), bf16),
            vm((count, rows, 2 * span), f32),
            vm((count, rows, 2 * span), bf16),
            vm((3, count, rows, 2 * span), bf16),
            vm((exp_here * rows, cols), bf16),
            vm((count, rows, cols), f32),
            vm((count, rows, cols), bf16),
            vm((count, count, rows, cols), bf16),
            vm((count, rows, cols), bf16),
            vm((count, rows, span), f32),
            vm((count, rows, span), bf16),
            vm((3, count, rows, span), bf16),
            vm((count, rows, out_feats), bf16),
            vm((count, rows, out_feats), bf16),
            vm((rows, out_feats), f32),
            sem((2,)), sem((3,)), four, four, four, sem((count, 2)), four,
            grid4, grid4, grid4, grid4, grid4, grid4, three, three,
            four, sem((count, count)), sem((2, count)), four, three, three, four, four, sem((10 + 2 * chunks,)),
        ],
        compiler_params=pltpu.CompilerParams(collective_id=0, has_side_effects=True, vmem_limit_bytes=60 * 1024 * 1024),
    )(
        tokens, routes.T, shares.T, delta, bg, bu, bd,
        jnp.swapaxes(gl, 1, 2).reshape(span, feats), gr.reshape(span, cols),
        jnp.swapaxes(ul, 1, 2).reshape(span, feats), ur.reshape(span, cols),
        jnp.swapaxes(dl, 1, 2).reshape(span, cols), dr.reshape(span, out_feats),
    )


def shards(
    tokens,
    routes,
    gate_weights,
    delta_of,
    base_gate,
    base_up,
    base_down,
    gate_left,
    gate_right,
    up_left,
    up_right,
    down_left,
    down_right,
):
    if lax.axis_size("narrow") == PLANE and lax.axis_size("wide") == PLANE:
        return fused(
            tokens, routes, gate_weights, delta_of, base_gate, base_up, base_down,
            gate_left, gate_right, up_left, up_right, down_left, down_right,
        )
    exp_here, _, rank = gate_left.shape
    experts = delta_of.shape[0]
    mine = lax.axis_index("wide")
    bf16 = jnp.bfloat16

    expert_ids = lax.broadcasted_iota(jnp.int32, (1, 1, experts), 2)
    named = routes[:, :, None] == expert_ids
    delta_ids = jnp.sum(jnp.where(named, delta_of[None, None, :], 0), axis=2)
    weight_of = jnp.sum(
        jnp.where(delta_ids[:, :, None] == expert_ids, gate_weights[:, :, None], 0.0), axis=1
    )
    weights = lax.all_gather(weight_of, "wide", axis=0, tiled=True)
    weights = lax.dynamic_slice_in_dim(weights, mine * exp_here, exp_here, axis=1)

    rows = lax.all_gather(tokens, "wide", axis=0, tiled=True)
    full = lax.all_gather(rows, "narrow", axis=1, tiled=True)
    depth = base_gate.shape[0]
    part = lax.dynamic_slice_in_dim(full, mine * depth, depth, axis=1)

    base_both = jnp.concatenate([base_gate, base_up], axis=1)
    both = lax.psum(dot32(part, base_both), "wide")
    columns = base_gate.shape[1]

    lefts = jnp.concatenate([gate_left, up_left], axis=0)
    low = lax.psum(jnp.einsum("td,edr->ter", rows, lefts, preferred_element_type=jnp.float32), "narrow")
    low = low.astype(bf16)

    mixed = 0.0
    thin = []
    for e in range(exp_here):
        gate = both[:, :columns] + dot32(low[:, e], gate_right[e])
        up = both[:, columns:] + dot32(low[:, exp_here + e], up_right[e])
        hidden = jax.nn.silu(gate) * up * weights[:, e : e + 1]
        mixed = mixed + hidden
        thin.append(dot32(hidden.astype(bf16), down_left[e]))
    mixed = lax.psum(mixed, "wide").astype(bf16)
    mixed_full = lax.all_gather(mixed, "narrow", axis=1, tiled=True)
    depth = base_down.shape[0]
    mixed_part = lax.dynamic_slice_in_dim(mixed_full, mine * depth, depth, axis=1)
    thin = lax.psum(jnp.concatenate(thin, axis=1), "narrow").astype(bf16)
    out = dot32(mixed_part, base_down) + dot32(thin, down_right.reshape(exp_here * rank, -1))
    out = lax.psum_scatter(out, "wide", scatter_dimension=0, tiled=True)
    return out.astype(bf16)


def solution(mesh):
    return jax.shard_map(
        shards,
        mesh=mesh,
        in_specs=(
            P(("groups", "wide"), "narrow"),
            P(("groups", "wide"), None),
            P(("groups", "wide"), None),
            P(),
            P("wide", "narrow"),
            P("wide", "narrow"),
            P("wide", "narrow"),
            P("wide", "narrow", None),
            P("wide", None, "narrow"),
            P("wide", "narrow", None),
            P("wide", None, "narrow"),
            P("wide", "narrow", None),
            P("wide", None, "narrow"),
        ),
        out_specs=P(("groups", "wide"), "narrow"),
        check_vma=False,
    )
```
